512 devices in a mesh: seg: 64 (over z, x), sub: 8 (over y, core).
Axes of the slice: x: 4, y: 4, z: 16, core: 2. Of those that a mesh axis runs over, the one named last changes fastest.
Arguments:
- near_blocks: bfloat16 [1024, 10, 256, 256], P(('seg', 'sub')), may hold values from -0.375 to 0.375
- sample_cols: bfloat16 [262144, 256], P(('seg', 'sub')), may hold values from -6 to 6
- near_list: int32 [1024, 10], P(('seg', 'sub')), may hold values from -1 to 1023, as said below
- row_basis_t: bfloat16 [1024, 64, 256], P(('seg', 'sub')), may hold values from -0.75 to 0.75
- col_basis_t: bfloat16 [1024, 64, 256], P(('seg', 'sub')), may hold values from -0.375 to 0.375
- couplings: bfloat16 [64, 8, 64, 64, 128], P('seg', 'sub'), may hold values from -0.125 to 0.125
- far_source: int32 [64, 8, 64, 2], P('seg', 'sub'), may hold values from 0 to 2
- far_dest: int32 [64, 8, 64, 2], P('seg', 'sub'), may hold values from 0 to 1
Outputs:
- samples: bfloat16 [262144, 256], P(('seg', 'sub'))
- segment_factor: float32 [16384, 256], P('seg')
- transfers: bfloat16 [64, 3, 256, 256], P('seg')
The draws below stay inside these ranges and needn't reach their ends.
Inputs may be any that keep to these rules, and one draw needn't show every extreme that they name: `near_list`: entry 0 of every list is the leaf itself; -1 marks padding and stands only after the real entries; every other entry names a leaf held by the same device or by the device just before or just after it in the order of seg, then sub. `far_source`: entry [s', u, s, c] is the local leaf of device (s', u) whose far projection fills slot c toward device (s, u); the value 2 marks an empty slot. `far_dest`: entry [s, u, s', c] is the local leaf of device (s, u) that slot c from device (s', u) serves.
All inputs are finite; a program needn't handle non-finite values.
Results may differ from the reference program's by a relative error of at most 0.013.
Values may be sent and summed in bfloat16 or wider, within the bound.
A program may use at most 64 MiB of HBM per device.

```python
import jax
import jax.numpy as jnp
from jax import lax

LEAF = 256
SAMP = 256
RANK = 64
NEAR = 10
CAP = 2
LEVELS = 3
LEAF_DEV = 2
LEAVES = 1024
FAR_SLOTS = 128
N_SEG = 64
N_SUB = 8
DEVICES = 512


def draw_near_list(key, part):
    leaf_ids = jnp.arange(LEAVES, dtype=jnp.int32)
    device_ids = leaf_ids // LEAF_DEV
    offsets = jax.random.randint(jax.random.fold_in(key, 11), (LEAVES, NEAR), 0, 3 * LEAF_DEV)
    candidate = (device_ids[:, None] - 1) * LEAF_DEV + offsets
    in_range = (candidate >= 0) & (candidate < LEAVES)
    candidate = jnp.where(in_range, candidate, leaf_ids[:, None])
    list_length = jax.random.randint(jax.random.fold_in(key, 12), (LEAVES,), NEAR // 2 + 1, NEAR + 1)
    list_length = jnp.where(leaf_ids == 0, NEAR - 1, list_length)
    slot_ids = jnp.arange(NEAR, dtype=jnp.int32)[None, :]
    candidate = jnp.where(slot_ids == 0, leaf_ids[:, None], candidate)
    return jnp.where(slot_ids < list_length[:, None], candidate, -1).astype(jnp.int32)


def place_ends(array, key, low, largest):
    index_at = [jax.random.randint(jax.random.fold_in(key, axis), (), 0, length) for axis, length in enumerate(array.shape)]
    longest = array.shape.index(max(array.shape))
    neighbour = index_at[:longest] + [(index_at[longest] + 1) % array.shape[longest]] + index_at[longest + 1:]
    return array.at[tuple(index_at)].set(low).at[tuple(neighbour)].set(largest)


def block_scale(key, dims, cuts, low, high):
    factor_of, own = 1.0, jax.random.fold_in(key, 6)
    for axis_at, shards_of in cuts:
        draws = jnp.exp(jax.random.uniform(jax.random.fold_in(own, axis_at), (shards_of,), jnp.float32, low / len(cuts), high / len(cuts)))
        factor_of = factor_of * jnp.repeat(draws, dims[axis_at] // shards_of).reshape([-1 if axis == axis_at else 1 for axis in range(len(dims))])
    return factor_of


def noise(stream_key, shape, width, limit, pieces=(), held_as=jnp.bfloat16):
    array = width * jax.random.normal(stream_key, shape, jnp.float32)
    if pieces:
        array = array * block_scale(stream_key, shape, pieces, -0.22, 0.18)
    return jnp.clip(array, -limit, limit).astype(held_as)


def setup_inputs(seed: int = 0) -> dict:
    streams_of = jax.random.split(jax.random.key(seed), 9)
    return {
        "near_blocks": noise(streams_of[0], (LEAVES, NEAR, LEAF, LEAF), LEAF ** -0.5, 0.375, ((0, 512),)),
        "sample_cols": noise(streams_of[1], (LEAVES * LEAF, SAMP), 1.0, 6.0, ((0, 512),)),
        "near_list": draw_near_list(jax.random.fold_in(streams_of[8], 71), 0),
        "row_basis_t": noise(streams_of[3], (LEAVES, RANK, LEAF), RANK ** -0.5, 0.75, ((0, 512),)),
        "col_basis_t": noise(streams_of[4], (LEAVES, RANK, LEAF), LEAF ** -0.5, 0.375, ((0, 512),)),
        "couplings": noise(streams_of[5], (N_SEG, N_SUB, N_SEG, RANK, CAP * RANK), (RANK * FAR_SLOTS // 4) ** -0.5, 0.125, ((0, 64), (1, 8))),
        "far_source": place_ends(jax.random.randint(streams_of[6], (N_SEG, N_SUB, N_SEG, CAP), 0, LEAF_DEV + 1), jax.random.fold_in(streams_of[6], 1), 0, LEAF_DEV).astype(jnp.int32),
        "far_dest": place_ends(jax.random.randint(streams_of[7], (N_SEG, N_SUB, N_SEG, CAP), 0, LEAF_DEV), jax.random.fold_in(streams_of[7], 1), 0, LEAF_DEV - 1).astype(jnp.int32),
    }


def leaf_adjacent(block_set, index_collection, random_cols):
    usable = index_collection >= 0
    chosen = random_cols[jnp.where(usable, index_collection, 0)]
    chosen = jnp.where(usable[:, None, None], chosen, jnp.zeros_like(chosen))
    return jnp.einsum('kab,kbs->as', block_set.astype(jnp.float32), chosen.astype(jnp.float32), precision=lax.Precision.HIGHEST)

def reference(near_blocks, sample_cols, near_list, row_basis_t, col_basis_t, couplings, far_source, far_dest):
    random_cols = sample_cols.reshape(LEAVES, LEAF, SAMP)
    basis_projector = jnp.einsum('jra,jas->jrs', col_basis_t.astype(jnp.float32), random_cols.astype(jnp.float32), precision=lax.Precision.HIGHEST).astype(jnp.bfloat16)
    near_part = lax.map(lambda bundle: leaf_adjacent(bundle[0], bundle[1], random_cols), (near_blocks, near_list))
    source_t = jnp.transpose(far_source, (2, 1, 0, 3))
    owner_base = (jnp.arange(N_SEG, dtype=jnp.int32)[None, None, :, None] * N_SUB + jnp.arange(N_SUB, dtype=jnp.int32)[None, :, None, None]) * LEAF_DEV
    global_leaf = (owner_base + source_t).astype(jnp.int32).reshape(DEVICES, N_SEG, CAP)
    occupied = (source_t < LEAF_DEV).reshape(DEVICES, N_SEG, CAP)
    target_leaf = far_dest.reshape(DEVICES, N_SEG, CAP)
    coupling_set = couplings.reshape(DEVICES, N_SEG, RANK, CAP, RANK)

    def remote_processor(bundle):
        leaf_ids, alive, targets, coupling_one = bundle
        slot_data = basis_projector[jnp.where(alive, leaf_ids, 0)]
        slot_data = jnp.where(alive[:, :, None, None], slot_data, jnp.zeros_like(slot_data))
        routing = (targets[:, :, None] == jnp.arange(LEAF_DEV, dtype=jnp.int32)[None, None, :]).astype(jnp.float32)
        products = jnp.einsum('pacb,pcbs->pcas', coupling_one.astype(jnp.float32), slot_data.astype(jnp.float32), precision=lax.Precision.HIGHEST)
        return jnp.einsum('pcas,pcl->las', products, routing, precision=lax.Precision.HIGHEST)
    far_coeff = lax.map(remote_processor, (global_leaf, occupied, target_leaf, coupling_set)).astype(jnp.bfloat16)
    far_coeff = far_coeff.reshape(LEAVES, RANK, SAMP)
    distant_portion = jnp.einsum('jra,jrs->jas', row_basis_t.astype(jnp.float32), far_coeff.astype(jnp.float32), precision=lax.Precision.HIGHEST)
    samples = (near_part + distant_portion).astype(jnp.bfloat16).reshape(LEAVES * LEAF, SAMP)
    sample_rows = samples.reshape(DEVICES, LEAF_DEV * LEAF, SAMP).astype(jnp.float32)
    gram_local = jnp.einsum('dns,dnt->dst', sample_rows, sample_rows, precision=lax.Precision.HIGHEST)
    seg_gram = gram_local.reshape(N_SEG, N_SUB, SAMP, SAMP).sum(axis=1) / (N_SUB * LEAF_DEV * LEAF)
    gram_levels = [seg_gram]
    current = seg_gram
    for segment_position_index in range(LEVELS):
        paired = current.reshape(-1, 2, SAMP, SAMP)
        current = (paired[:, 0] + paired[:, 1]) * 0.5
        gram_levels.append(jnp.repeat(current, 2 ** (segment_position_index + 1), axis=0))
    stacked = jnp.stack(gram_levels, axis=1)
    triangles = jnp.linalg.cholesky(stacked)
    segment_factor = jnp.swapaxes(triangles[:, 0], 1, 2).reshape(N_SEG * SAMP, SAMP)
    solved = jax.vmap(jax.vmap(lambda upper_one, lower_one: jax.scipy.linalg.solve_triangular(upper_one, lower_one, lower=True)))(triangles[:, 1:], triangles[:, :-1])
    transfers = jnp.swapaxes(solved, 2, 3).astype(jnp.bfloat16)
    return (samples, segment_factor, transfers)
```

```python
import jax
import jax.numpy as jnp
from jax import lax
from jax.experimental import pallas as pl
from jax.experimental.pallas import tpu as pltpu
from jax.sharding import PartitionSpec as P

LEVELS = 3

BLOCK = 32
GROUP = 8


def dot32(a, b, dims):
    return lax.dot_general(
        a, b, (dims, ((), ())), precision=lax.Precision.HIGHEST, preferred_element_type=jnp.float32
    )


def eliminate(blocks):
    size = blocks[0].shape[0]
    rows = lax.broadcasted_iota(jnp.int32, (size, size), 0)
    cols = lax.broadcasted_iota(jnp.int32, (size, size), 1)
    eye = (rows == cols).astype(jnp.float32)
    sub = lax.broadcasted_iota(jnp.int32, (GROUP, 1), 0)
    states = []
    for d in blocks:
        x = jnp.concatenate([d, eye], axis=1)
        states.append([x[g * GROUP : (g + 1) * GROUP] for g in range(size // GROUP)])
    for k in range(size):
        own, r = divmod(k, GROUP)
        for x in states:
            line = x[own][r : r + 1, :]
            scale = lax.rsqrt(line[:, k : k + 1])
            line = line * scale
            for g in range(own, size // GROUP):
                factor = x[g][:, k : k + 1] * scale
                if g == own:
                    below = x[g] - jnp.where(sub > r, factor, 0.0) * line
                    x[g] = jnp.where(sub == r, line, below)
                else:
                    x[g] = x[g] - factor * line
    out = []
    for x in states:
        x = jnp.concatenate(x, axis=0)
        out.append((jnp.where(rows <= cols, x[:, :size], 0.0), x[:, size:]))
    return out


def factor_kernel(gram_ref, factor_ref, transfer_ref, work, upper):
    count, n, _ = work.shape
    lanes = lax.broadcasted_iota(jnp.int32, (1, n), 1)
    work[...] = gram_ref[...]
    upper[...] = jnp.zeros_like(upper)
    for at in range(0, n, BLOCK):
        end = at + BLOCK
        inside = (lanes >= at) & (lanes < end)
        pairs = eliminate([work[i, at:end, at:end] for i in range(count)])
        for i in range(count):
            r_block, v_block = pairs[i]
            panel = dot32(v_block, work[i, at:end, :], ((1,), (0,)))
            upper[i, at:end, :] = jnp.where(lanes >= end, panel, 0.0)
            upper[i, at:end, at:end] = r_block
            work[i, at:end, :] = jnp.where(lanes < at, panel, 0.0)
            work[i, at:end, at:end] = v_block
            if end < n:
                step = jnp.where(lanes < at, panel, upper[i, at:end, :])
                step = jnp.where(inside, work[i, at:end, :], step)
                rest = jnp.where(inside, 0.0, work[i, end:, :])
                work[i, end:, :] = rest - dot32(panel[:, end:], step, ((0,), (0,)))
    factor_ref[...] = upper[0]
    for i in range(1, count):
        transfer_ref[i - 1] = dot32(upper[i - 1], work[i], ((1,), (1,))).astype(jnp.bfloat16)


def factors(stacked):
    count, n, _ = stacked.shape
    return pl.pallas_call(
        factor_kernel,
        out_shape=(
            jax.ShapeDtypeStruct((n, n), jnp.float32),
            jax.ShapeDtypeStruct((count - 1, n, n), jnp.bfloat16),
        ),
        in_specs=[pl.BlockSpec(memory_space=pltpu.VMEM)],
        out_specs=[pl.BlockSpec(memory_space=pltpu.VMEM)] * 2,
        scratch_shapes=[
            pltpu.VMEM((count, n, n), jnp.float32),
            pltpu.VMEM((count, n, n), jnp.float32),
        ],
    )(stacked)


FAR_UNROLL = 4


def far_kernel(
    source_ref, dest_ref, gathered_ref, coupling_ref, basis_ref, near_ref, samples_ref, gram_ref
):
    leaf_count, rank, leaf_rows = basis_ref.shape
    seg_count = coupling_ref.shape[0]
    slots = coupling_ref.shape[2] // rank
    width = gathered_ref.shape[2]
    lane = lax.broadcasted_iota(jnp.int32, (1, slots * rank), 1) // rank

    def step(index, total):
        left, right = [], []
        for part in range(FAR_UNROLL):
            seg = index * FAR_UNROLL + part
            key = jnp.full((1, slots * rank), -1, jnp.int32)
            for slot in range(slots):
                source = source_ref[seg * slots + slot]
                served = jnp.where(source < leaf_count, dest_ref[seg * slots + slot], -1)
                key = jnp.where(lane == slot, served, key)
                start = pl.multiple_of(jnp.minimum(source, leaf_count - 1) * rank, rank)
                right.append(gathered_ref[seg, pl.ds(start, rank), :])
            block = coupling_ref[seg]
            left.append(
                jnp.concatenate(
                    [jnp.where(key == leaf, block, jnp.zeros_like(block)) for leaf in range(leaf_count)],
                    axis=0,
                )
            )
        return total + jnp.dot(
            jnp.concatenate(left, axis=1),
            jnp.concatenate(right, axis=0),
            preferred_element_type=jnp.float32,
        )

    total = lax.fori_loop(
        0, seg_count // FAR_UNROLL, step, jnp.zeros((leaf_count * rank, width), jnp.float32)
    )
    coeff = total.astype(jnp.bfloat16)
    for leaf in range(leaf_count):
        rows = slice(leaf * leaf_rows, (leaf + 1) * leaf_rows)
        far = lax.dot_general(
            basis_ref[leaf],
            coeff[leaf * rank : (leaf + 1) * rank],
            (((0,), (0,)), ((), ())),
            preferred_element_type=jnp.float32,
        )
        samples_ref[rows, :] = (near_ref[rows, :] + far).astype(jnp.bfloat16)
    samples = samples_ref[...]
    gram_ref[...] = lax.dot_general(
        samples, samples, (((0,), (0,)), ((), ())), preferred_element_type=jnp.float32
    ).astype(gram_ref.dtype)


def far_and_gram(source, dest, gathered, coupling, basis, near):
    rows, width = near.shape
    smem, vmem = pl.BlockSpec(memory_space=pltpu.SMEM), pl.BlockSpec(memory_space=pltpu.VMEM)
    return pl.pallas_call(
        far_kernel,
        out_shape=(
            jax.ShapeDtypeStruct((rows, width), jnp.bfloat16),
            jax.ShapeDtypeStruct((width, width), jnp.bfloat16),
        ),
        in_specs=[smem, smem, vmem, vmem, vmem, vmem],
        out_specs=[vmem, vmem],
        compiler_params=pltpu.CompilerParams(vmem_limit_bytes=32 * 2**20),
    )(source, dest, gathered, coupling, basis, near)


def padded(value, sides, width):
    for axis, dim in sides:
        size, length = (lax.axis_size(axis), value.shape[dim])
        up = [(i, (i + 1) % size) for i in range(size - 1)]
        down = [(j, i) for i, j in up]
        last = lax.slice_in_dim(value, length - width, length, axis=dim)
        leading = lax.slice_in_dim(value, 0, width, axis=dim)
        before = lax.ppermute(last, axis, up)
        after = lax.ppermute(leading, axis, down)
        value = jnp.concatenate([before, value, after], axis=dim)
    return value


def from_partner(value, axis, distance):
    mask = 2**distance
    pairs = [(source, source ^ mask) for source in range(lax.axis_size(axis))]
    return lax.ppermute(value, axis, pairs)


def paired_sum(value, axis, distance):
    partner = from_partner(value, axis, distance)
    return value.astype(jnp.float32) + partner.astype(jnp.float32)


def body(
    near_blocks, sample_cols, near_list, row_basis_t, col_basis_t, couplings, far_source, far_dest
):
    leaf_count, near_count, leaf_rows, _ = near_blocks.shape
    sample_width = sample_cols.shape[1]
    rank_width = row_basis_t.shape[1]
    seg_count = lax.axis_size("seg")
    slot_number_count = far_source.shape[3]
    random_cols = sample_cols.reshape(leaf_count, leaf_rows, sample_width)
    basis_projector = jnp.einsum(
        "jra,jas->jrs", col_basis_t, random_cols, preferred_element_type=jnp.float32
    ).astype(jnp.bfloat16)
    source_rows = jnp.swapaxes(far_source[0, 0], 0, 1).astype(jnp.bfloat16)
    source_rows = jnp.pad(
        source_rows, ((0, 16 - slot_number_count), (0, sample_width - seg_count))
    )
    packed = jnp.concatenate(
        [basis_projector.reshape(leaf_count * rank_width, sample_width), source_rows], axis=0
    )
    gathered = lax.all_gather(packed, "seg")
    sources = gathered[:, leaf_count * rank_width : leaf_count * rank_width + slot_number_count, :]
    sources = lax.dynamic_slice_in_dim(sources, lax.axis_index("seg"), 1, axis=2)
    sources = sources.astype(jnp.int32).reshape(seg_count * slot_number_count)
    extended = padded(sample_cols, ((("seg", "sub"), 0),), leaf_count * leaf_rows)
    extended = extended.reshape(3 * leaf_count, leaf_rows, sample_width)
    base_leaf = (lax.axis_index(("seg", "sub")) - 1) * leaf_count
    usable = near_list >= 0
    position = jnp.where(usable, near_list - base_leaf, 0)
    chosen = extended[position]
    chosen = jnp.where(usable[:, :, None, None], chosen, jnp.zeros_like(chosen))
    near_part = jnp.einsum(
        "lkab,lkbs->las", near_blocks, chosen, preferred_element_type=jnp.float32
    )
    samples, gram_local = far_and_gram(
        sources,
        far_dest.reshape(seg_count * slot_number_count),
        gathered,
        couplings[0, 0],
        row_basis_t,
        near_part.reshape(leaf_count * leaf_rows, sample_width),
    )
    row_total = lax.axis_size("sub") * leaf_count * leaf_rows
    current = gram_local
    for distance in range((lax.axis_size("sub") - 1).bit_length()):
        total = paired_sum(current, "sub", distance)
        current = total.astype(jnp.bfloat16)
    gram_levels = [total / row_total]
    for distance in range(LEVELS):
        total = paired_sum(gram_levels[-1].astype(jnp.bfloat16), "seg", distance) * 0.5
        gram_levels.append(total)
    segment_factor, transfers = factors(jnp.stack(gram_levels))
    return (samples, segment_factor, transfers[None])


def solution(mesh):
    in_specs = (
        P(("seg", "sub"), None, None, None),
        P(("seg", "sub"), None),
        P(("seg", "sub"), None),
        P(("seg", "sub"), None, None),
        P(("seg", "sub"), None, None),
        P("seg", "sub", None, None, None),
        P("seg", "sub", None, None),
        P("seg", "sub", None, None),
    )
    out_specs = (P(("seg", "sub"), None), P("seg", None), P("seg", None, None, None))
    return jax.shard_map(body, mesh=mesh, in_specs=in_specs, out_specs=out_specs, check_vma=False)
```

```python
import jax
import jax.numpy as jnp
from jax import lax
from jax.experimental import pallas as pl
from jax.experimental.pallas import tpu as pltpu
from jax.sharding import PartitionSpec as P

LEVELS = 3

BLOCK = 32
GROUP = 8


def dot32(a, b, dims):
    return lax.dot_general(
        a, b, (dims, ((), ())), precision=lax.Precision.HIGHEST, preferred_element_type=jnp.float32
    )


def eliminate(blocks):
    size = blocks[0].shape[0]
    rows = lax.broadcasted_iota(jnp.int32, (size, size), 0)
    cols = lax.broadcasted_iota(jnp.int32, (size, size), 1)
    eye = (rows == cols).astype(jnp.float32)
    sub = lax.broadcasted_iota(jnp.int32, (GROUP, 1), 0)
    states = []
    for d in blocks:
        x = jnp.concatenate([d, eye], axis=1)
        states.append([x[g * GROUP : (g + 1) * GROUP] for g in range(size // GROUP)])
    for k in range(size):
        own, r = divmod(k, GROUP)
        for x in states:
            line = x[own][r : r + 1, :]
            scale = lax.rsqrt(line[:, k : k + 1])
            line = line * scale
            for g in range(own, size // GROUP):
                factor = x[g][:, k : k + 1] * scale
                if g == own:
                    below = x[g] - jnp.where(sub > r, factor, 0.0) * line
                    x[g] = jnp.where(sub == r, line, below)
                else:
                    x[g] = x[g] - factor * line
    out = []
    for x in states:
        x = jnp.concatenate(x, axis=0)
        out.append((jnp.where(rows <= cols, x[:, :size], 0.0), x[:, size:]))
    return out


def factor_kernel(gram_ref, factor_ref, transfer_ref, work, upper):
    count, n, _ = work.shape
    lanes = lax.broadcasted_iota(jnp.int32, (1, n), 1)
    work[...] = gram_ref[...]
    upper[...] = jnp.zeros_like(upper)
    for at in range(0, n, BLOCK):
        end = at + BLOCK
        inside = (lanes >= at) & (lanes < end)
        pairs = eliminate([work[i, at:end, at:end] for i in range(count)])
        for i in range(count):
            r_block, v_block = pairs[i]
            panel = dot32(v_block, work[i, at:end, :], ((1,), (0,)))
            upper[i, at:end, :] = jnp.where(lanes >= end, panel, 0.0)
            upper[i, at:end, at:end] = r_block
            work[i, at:end, :] = jnp.where(lanes < at, panel, 0.0)
            work[i, at:end, at:end] = v_block
            if end < n:
                step = jnp.where(lanes < at, panel, upper[i, at:end, :])
                step = jnp.where(inside, work[i, at:end, :], step)
                rest = jnp.where(inside, 0.0, work[i, end:, :])
                work[i, end:, :] = rest - dot32(panel[:, end:], step, ((0,), (0,)))
    factor_ref[...] = upper[0]
    for i in range(1, count):
        transfer_ref[i - 1] = dot32(upper[i - 1], work[i], ((1,), (1,))).astype(jnp.bfloat16)


def factors(stacked):
    count, n, _ = stacked.shape
    return pl.pallas_call(
        factor_kernel,
        out_shape=(
            jax.ShapeDtypeStruct((n, n), jnp.float32),
            jax.ShapeDtypeStruct((count - 1, n, n), jnp.bfloat16),
        ),
        in_specs=[pl.BlockSpec(memory_space=pltpu.VMEM)],
        out_specs=[pl.BlockSpec(memory_space=pltpu.VMEM)] * 2,
        scratch_shapes=[
            pltpu.VMEM((count, n, n), jnp.float32),
            pltpu.VMEM((count, n, n), jnp.float32),
        ],
    )(stacked)


SIDE = 4
PLUS, MINUS = 0, 1


def gather_kernel(own_ref, out_ref, own_sem, near_sems, ring_sems, line_sems, relay_sems):
    seg_count, rows, _ = out_ref.shape
    depth = seg_count // SIDE
    half = depth // 2
    me = lax.axis_index("seg")
    z, x = me // SIDE, lax.rem(me, SIDE)
    early = pl.ds(0, rows // 48 * 16)
    late = pl.ds(rows // 48 * 16, rows - rows // 48 * 16)
    sign = (1, -1)
    reach = (half, half - 1)

    def place(dz, dx):
        return lax.rem(z + dz + depth, depth) * SIDE + lax.rem(x + dx + SIDE, SIDE)

    def send(dz, dx, part, sems, target, own):
        source = own_ref.at[part] if own else out_ref.at[place(dz, dx), part]
        return pltpu.make_async_remote_copy(
            src_ref=source,
            dst_ref=out_ref.at[place(dz, dx), part],
            send_sem=sems.at[0],
            recv_sem=sems.at[1],
            device_id={"seg": target},
            device_id_type=pl.DeviceIdType.MESH,
        )

    def along_x(way):
        return place(0, sign[way])

    def along_z(way):
        return place(sign[way], 0)

    def near(way):
        return send(0, 0, early, near_sems.at[way], along_x(way), True)

    def near_relay():
        return send(0, -1, early, near_sems.at[2], along_x(PLUS), False)

    def ring(stream, way, hop, own=False):
        part, dx = (late, 0) if stream == SIDE else (early, stream)
        return send(
            -sign[way] * (hop - 1), dx, part, ring_sems.at[stream, way, hop], along_z(way), own
        )

    def line(hop, way, side, own=False):
        return send(-sign[way] * hop, 0, late, line_sems.at[hop, way, side], along_x(side), own)

    def relay(hop, way, side):
        return send(-sign[way] * hop, -sign[side], late, relay_sems.at[hop, way], along_x(side), False)

    def pass_on(hop, way, side):
        line(hop, way, side).wait_recv()
        relay(hop, way, side).start()

    def advance(stream, way, hop, further):
        ring(stream, way, hop).wait_recv()
        if further:
            ring(stream, way, hop + 1).start()

    def turn(hop, ways, further, streams):
        for way in ways:
            advance(SIDE, way, hop, way in further)
            for side in (PLUS, MINUS):
                line(hop, way, side).start()
        for stream in streams:
            for way in ways:
                advance(stream, way, hop, way in further)

    barrier = pltpu.get_barrier_semaphore()
    for way in (PLUS, MINUS):
        for target in (along_x(way), along_z(way)):
            pl.semaphore_signal(
                barrier, inc=1, device_id={"seg": target}, device_id_type=pl.DeviceIdType.MESH
            )
    pl.semaphore_wait(barrier, 4)

    keep = pltpu.make_async_copy(own_ref, out_ref.at[me], own_sem)
    keep.start()
    for way in (PLUS, MINUS):
        near(way).start()
        ring(SIDE, way, 1, True).start()
    for way in (PLUS, MINUS):
        ring(0, way, 1, True).start()
        line(0, PLUS, way, True).start()
    both = (PLUS, MINUS)
    for way, stream in ((PLUS, SIDE - 1), (MINUS, 1)):
        near(way).wait_recv()
        if way == PLUS:
            near_relay().start()
        for side in both:
            ring(stream, side, 1).start()
    turn(1, both, both, (0, SIDE - 1, 1))
    near_relay().wait_recv()
    for side in both:
        ring(2, side, 1).start()
    pass_on(0, PLUS, PLUS)
    for way in both:
        advance(2, way, 1, True)

    def middle(hop, carry):
        turn(hop, both, both, (0, SIDE - 1, 1, 2))
        for way in both:
            pass_on(hop - 1, way, way)
        return carry

    lax.fori_loop(2, half - 1, middle, 0)
    turn(half - 1, both, (PLUS,), (0, SIDE - 1, 1, 2))
    for way in both:
        pass_on(half - 2, way, way)
    turn(half, (PLUS,), (), (0, SIDE - 1, 1, 2))
    for way in both:
        pass_on(half - 1, way, way)
    pass_on(half, PLUS, MINUS)

    def finish(hop, way, side):
        line(hop, way, 1 - side).wait_recv()
        relay(hop, way, side).wait_recv()
        for out in both:
            line(hop, way, out).wait_send()
        relay(hop, way, side).wait_send()

    def drain(hop, carry):
        for way in both:
            finish(hop, way, way)
            for stream in range(SIDE + 1):
                ring(stream, way, hop).wait_send()
        return carry

    finish(0, PLUS, PLUS)
    lax.fori_loop(1, half, drain, 0)
    finish(half, PLUS, MINUS)
    for stream in range(SIDE + 1):
        ring(stream, PLUS, half).wait_send()
    for way in both:
        near(way).wait_send()
    near_relay().wait_send()
    keep.wait()


def gather_segments(value):
    rows, width = value.shape
    seg_count = lax.axis_size("seg")
    half = seg_count // SIDE // 2
    dma = pltpu.SemaphoreType.DMA
    return pl.pallas_call(
        gather_kernel,
        out_shape=jax.ShapeDtypeStruct((seg_count, rows, width), value.dtype),
        in_specs=[pl.BlockSpec(memory_space=pltpu.VMEM)],
        out_specs=pl.BlockSpec(memory_space=pltpu.VMEM),
        scratch_shapes=[
            dma,
            dma((3, 2)),
            dma((SIDE + 1, 2, half + 1, 2)),
            dma((half + 1, 2, 2, 2)),
            dma((half + 1, 2, 2)),
        ],
        compiler_params=pltpu.CompilerParams(
            collective_id=0, has_side_effects=True, vmem_limit_bytes=32 * 2**20
        ),
    )(value)


FAR_UNROLL = 4


def far_kernel(
    source_ref, dest_ref, gathered_ref, coupling_ref, basis_ref, near_ref, samples_ref, gram_ref
):
    leaf_count, rank, leaf_rows = basis_ref.shape
    seg_count = coupling_ref.shape[0]
    slots = coupling_ref.shape[2] // rank
    width = gathered_ref.shape[2]
    lane = lax.broadcasted_iota(jnp.int32, (1, slots * rank), 1) // rank

    def step(index, total):
        left, right = [], []
        for part in range(FAR_UNROLL):
            seg = index * FAR_UNROLL + part
            key = jnp.full((1, slots * rank), -1, jnp.int32)
            for slot in range(slots):
                source = source_ref[seg * slots + slot]
                served = jnp.where(source < leaf_count, dest_ref[seg * slots + slot], -1)
                key = jnp.where(lane == slot, served, key)
                start = pl.multiple_of(jnp.minimum(source, leaf_count - 1) * rank, rank)
                right.append(gathered_ref[seg, pl.ds(start, rank), :])
            block = coupling_ref[seg]
            left.append(
                jnp.concatenate(
                    [jnp.where(key == leaf, block, jnp.zeros_like(block)) for leaf in range(leaf_count)],
                    axis=0,
                )
            )
        return total + jnp.dot(
            jnp.concatenate(left, axis=1),
            jnp.concatenate(right, axis=0),
            preferred_element_type=jnp.float32,
        )

    total = lax.fori_loop(
        0, seg_count // FAR_UNROLL, step, jnp.zeros((leaf_count * rank, width), jnp.float32)
    )
    coeff = total.astype(jnp.bfloat16)
    for leaf in range(leaf_count):
        rows = slice(leaf * leaf_rows, (leaf + 1) * leaf_rows)
        far = lax.dot_general(
            basis_ref[leaf],
            coeff[leaf * rank : (leaf + 1) * rank],
            (((0,), (0,)), ((), ())),
            preferred_element_type=jnp.float32,
        )
        samples_ref[rows, :] = (near_ref[rows, :] + far).astype(jnp.bfloat16)
    samples = samples_ref[...]
    gram_ref[...] = lax.dot_general(
        samples, samples, (((0,), (0,)), ((), ())), preferred_element_type=jnp.float32
    ).astype(gram_ref.dtype)


def far_and_gram(source, dest, gathered, coupling, basis, near):
    rows, width = near.shape
    smem, vmem = pl.BlockSpec(memory_space=pltpu.SMEM), pl.BlockSpec(memory_space=pltpu.VMEM)
    return pl.pallas_call(
        far_kernel,
        out_shape=(
            jax.ShapeDtypeStruct((rows, width), jnp.bfloat16),
            jax.ShapeDtypeStruct((width, width), jnp.bfloat16),
        ),
        in_specs=[smem, smem, vmem, vmem, vmem, vmem],
        out_specs=[vmem, vmem],
        compiler_params=pltpu.CompilerParams(vmem_limit_bytes=32 * 2**20),
    )(source, dest, gathered, coupling, basis, near)


def padded(value, sides, width):
    for axis, dim in sides:
        size, length = (lax.axis_size(axis), value.shape[dim])
        up = [(i, (i + 1) % size) for i in range(size - 1)]
        down = [(j, i) for i, j in up]
        last = lax.slice_in_dim(value, length - width, length, axis=dim)
        leading = lax.slice_in_dim(value, 0, width, axis=dim)
        before = lax.ppermute(last, axis, up)
        after = lax.ppermute(leading, axis, down)
        value = jnp.concatenate([before, value, after], axis=dim)
    return value


def from_partner(value, axis, distance):
    mask = 2**distance
    pairs = [(source, source ^ mask) for source in range(lax.axis_size(axis))]
    return lax.ppermute(value, axis, pairs)


def paired_sum(value, axis, distance):
    partner = from_partner(value, axis, distance)
    return value.astype(jnp.float32) + partner.astype(jnp.float32)


def body(
    near_blocks, sample_cols, near_list, row_basis_t, col_basis_t, couplings, far_source, far_dest
):
    leaf_count, near_count, leaf_rows, _ = near_blocks.shape
    sample_width = sample_cols.shape[1]
    rank_width = row_basis_t.shape[1]
    seg_count = lax.axis_size("seg")
    slot_number_count = far_source.shape[3]
    random_cols = sample_cols.reshape(leaf_count, leaf_rows, sample_width)
    basis_projector = jnp.einsum(
        "jra,jas->jrs", col_basis_t, random_cols, preferred_element_type=jnp.float32
    ).astype(jnp.bfloat16)
    source_rows = jnp.swapaxes(far_source[0, 0], 0, 1).astype(jnp.bfloat16)
    source_rows = jnp.pad(
        source_rows, ((0, 16 - slot_number_count), (0, sample_width - seg_count))
    )
    packed = jnp.concatenate(
        [basis_projector.reshape(leaf_count * rank_width, sample_width), source_rows], axis=0
    )
    gathered = gather_segments(packed)
    sources = gathered[:, leaf_count * rank_width : leaf_count * rank_width + slot_number_count, :]
    sources = lax.dynamic_slice_in_dim(sources, lax.axis_index("seg"), 1, axis=2)
    sources = sources.astype(jnp.int32).reshape(seg_count * slot_number_count)
    extended = padded(sample_cols, ((("seg", "sub"), 0),), leaf_count * leaf_rows)
    extended = extended.reshape(3 * leaf_count, leaf_rows, sample_width)
    base_leaf = (lax.axis_index(("seg", "sub")) - 1) * leaf_count
    usable = near_list >= 0
    position = jnp.where(usable, near_list - base_leaf, 0)
    chosen = extended[position]
    chosen = jnp.where(usable[:, :, None, None], chosen, jnp.zeros_like(chosen))
    near_part = jnp.einsum(
        "lkab,lkbs->las", near_blocks, chosen, preferred_element_type=jnp.float32
    )
    samples, gram_local = far_and_gram(
        sources,
        far_dest.reshape(seg_count * slot_number_count),
        gathered,
        couplings[0, 0],
        row_basis_t,
        near_part.reshape(leaf_count * leaf_rows, sample_width),
    )
    row_total = lax.axis_size("sub") * leaf_count * leaf_rows
    current = gram_local
    for distance in range((lax.axis_size("sub") - 1).bit_length()):
        total = paired_sum(current, "sub", distance)
        current = total.astype(jnp.bfloat16)
    gram_levels = [total / row_total]
    for distance in range(LEVELS):
        total = paired_sum(gram_levels[-1].astype(jnp.bfloat16), "seg", distance) * 0.5
        gram_levels.append(total)
    segment_factor, transfers = factors(jnp.stack(gram_levels))
    return (samples, segment_factor, transfers[None])


def solution(mesh):
    in_specs = (
        P(("seg", "sub"), None, None, None),
        P(("seg", "sub"), None),
        P(("seg", "sub"), None),
        P(("seg", "sub"), None, None),
        P(("seg", "sub"), None, None),
        P("seg", "sub", None, None, None),
        P("seg", "sub", None, None),
        P("seg", "sub", None, None),
    )
    out_specs = (P(("seg", "sub"), None), P("seg", None), P("seg", None, None, None))
    return jax.shard_map(body, mesh=mesh, in_specs=in_specs, out_specs=out_specs, check_vma=False)
```

```python
import functools

import jax
import jax.numpy as jnp
from jax import lax
from jax.experimental import pallas as pl
from jax.experimental.pallas import tpu as pltpu
from jax.sharding import PartitionSpec as P

LEVELS = 3

BLOCK = 32
GROUP = 8


def dot32(a, b, dims):
    return lax.dot_general(
        a, b, (dims, ((), ())), precision=lax.Precision.HIGHEST, preferred_element_type=jnp.float32
    )


def eliminate(blocks):
    size = blocks[0].shape[0]
    rows = lax.broadcasted_iota(jnp.int32, (size, size), 0)
    cols = lax.broadcasted_iota(jnp.int32, (size, size), 1)
    eye = (rows == cols).astype(jnp.float32)
    sub = lax.broadcasted_iota(jnp.int32, (GROUP, 1), 0)
    states = []
    for d in blocks:
        x = jnp.concatenate([d, eye], axis=1)
        states.append([x[g * GROUP : (g + 1) * GROUP] for g in range(size // GROUP)])
    for k in range(size):
        own, r = divmod(k, GROUP)
        for x in states:
            line = x[own][r : r + 1, :]
            scale = lax.rsqrt(line[:, k : k + 1])
            line = line * scale
            for g in range(own, size // GROUP):
                factor = x[g][:, k : k + 1] * scale
                if g == own:
                    below = x[g] - jnp.where(sub > r, factor, 0.0) * line
                    x[g] = jnp.where(sub == r, line, below)
                else:
                    x[g] = x[g] - factor * line
    out = []
    for x in states:
        x = jnp.concatenate(x, axis=0)
        out.append((jnp.where(rows <= cols, x[:, :size], 0.0), x[:, size:]))
    return out


def factor_kernel(gram_ref, factor_ref, transfer_ref, work, upper):
    count, n, _ = work.shape
    lanes = lax.broadcasted_iota(jnp.int32, (1, n), 1)
    work[...] = gram_ref[...].astype(jnp.float32)
    upper[...] = jnp.zeros_like(upper)
    for at in range(0, n, BLOCK):
        end = at + BLOCK
        inside = (lanes >= at) & (lanes < end)
        pairs = eliminate([work[i, at:end, at:end] for i in range(count)])
        for i in range(count):
            r_block, v_block = pairs[i]
            panel = dot32(v_block, work[i, at:end, :], ((1,), (0,)))
            upper[i, at:end, :] = jnp.where(lanes >= end, panel, 0.0)
            upper[i, at:end, at:end] = r_block
            work[i, at:end, :] = jnp.where(lanes < at, panel, 0.0)
            work[i, at:end, at:end] = v_block
            if end < n:
                step = jnp.where(lanes < at, panel, upper[i, at:end, :])
                step = jnp.where(inside, work[i, at:end, :], step)
                rest = jnp.where(inside, 0.0, work[i, end:, :])
                work[i, end:, :] = rest - dot32(panel[:, end:], step, ((0,), (0,)))
    factor_ref[...] = upper[0]
    for i in range(1, count):
        transfer_ref[i - 1] = dot32(upper[i - 1], work[i], ((1,), (1,))).astype(jnp.bfloat16)


def factors(stacked):
    count, n, _ = stacked.shape
    return pl.pallas_call(
        factor_kernel,
        out_shape=(
            jax.ShapeDtypeStruct((n, n), jnp.float32),
            jax.ShapeDtypeStruct((count - 1, n, n), jnp.bfloat16),
        ),
        in_specs=[pl.BlockSpec(memory_space=pltpu.VMEM)],
        out_specs=[pl.BlockSpec(memory_space=pltpu.VMEM)] * 2,
        scratch_shapes=[
            pltpu.VMEM((count, n, n), jnp.float32),
            pltpu.VMEM((count, n, n), jnp.float32),
        ],
    )(stacked)


SIDE = 4
PLUS, MINUS = 0, 1


def gather_kernel(own_ref, out_ref, own_sem, near_sems, ring_sems, line_sems, relay_sems):
    seg_count, rows, _ = out_ref.shape
    depth = seg_count // SIDE
    half = depth // 2
    me = lax.axis_index("seg")
    z, x = me // SIDE, lax.rem(me, SIDE)
    early = pl.ds(0, rows // 48 * 16)
    late = pl.ds(rows // 48 * 16, rows - rows // 48 * 16)
    sign = (1, -1)
    reach = (half, half - 1)

    def place(dz, dx):
        return lax.rem(z + dz + depth, depth) * SIDE + lax.rem(x + dx + SIDE, SIDE)

    def send(dz, dx, part, sems, target, own):
        source = own_ref.at[part] if own else out_ref.at[place(dz, dx), part]
        return pltpu.make_async_remote_copy(
            src_ref=source,
            dst_ref=out_ref.at[place(dz, dx), part],
            send_sem=sems.at[0],
            recv_sem=sems.at[1],
            device_id={"seg": target},
            device_id_type=pl.DeviceIdType.MESH,
        )

    def along_x(way):
        return place(0, sign[way])

    def along_z(way):
        return place(sign[way], 0)

    def near(way):
        return send(0, 0, early, near_sems.at[way], along_x(way), True)

    def near_relay():
        return send(0, -1, early, near_sems.at[2], along_x(PLUS), False)

    def ring(stream, way, hop, own=False):
        part, dx = (late, 0) if stream == SIDE else (early, stream)
        return send(
            -sign[way] * (hop - 1), dx, part, ring_sems.at[stream, way, hop], along_z(way), own
        )

    def line(hop, way, side, own=False):
        return send(-sign[way] * hop, 0, late, line_sems.at[hop, way, side], along_x(side), own)

    def relay(hop, way, side):
        return send(-sign[way] * hop, -sign[side], late, relay_sems.at[hop, way], along_x(side), False)

    def pass_on(hop, way, side):
        line(hop, way, side).wait_recv()
        relay(hop, way, side).start()

    def advance(stream, way, hop, further):
        ring(stream, way, hop).wait_recv()
        if further:
            ring(stream, way, hop + 1).start()

    def turn(hop, ways, further, streams):
        for way in ways:
            advance(SIDE, way, hop, way in further)
            for side in (PLUS, MINUS):
                line(hop, way, side).start()
        for stream in streams:
            for way in ways:
                advance(stream, way, hop, way in further)

    barrier = pltpu.get_barrier_semaphore()
    for way in (PLUS, MINUS):
        for target in (along_x(way), along_z(way)):
            pl.semaphore_signal(
                barrier, inc=1, device_id={"seg": target}, device_id_type=pl.DeviceIdType.MESH
            )
    pl.semaphore_wait(barrier, 4)

    keep = pltpu.make_async_copy(own_ref, out_ref.at[me], own_sem)
    keep.start()
    for way in (PLUS, MINUS):
        near(way).start()
        ring(SIDE, way, 1, True).start()
    for way in (PLUS, MINUS):
        ring(0, way, 1, True).start()
        line(0, PLUS, way, True).start()
    both = (PLUS, MINUS)
    for way, stream in ((PLUS, SIDE - 1), (MINUS, 1)):
        near(way).wait_recv()
        if way == PLUS:
            near_relay().start()
        for side in both:
            ring(stream, side, 1).start()
    turn(1, both, both, (0, SIDE - 1, 1))
    near_relay().wait_recv()
    for side in both:
        ring(2, side, 1).start()
    pass_on(0, PLUS, PLUS)
    for way in both:
        advance(2, way, 1, True)

    def middle(hop, carry):
        turn(hop, both, both, (0, SIDE - 1, 1, 2))
        for way in both:
            pass_on(hop - 1, way, way)
        return carry

    lax.fori_loop(2, half - 1, middle, 0)
    turn(half - 1, both, (PLUS,), (0, SIDE - 1, 1, 2))
    for way in both:
        pass_on(half - 2, way, way)
    turn(half, (PLUS,), (), (0, SIDE - 1, 1, 2))
    for way in both:
        pass_on(half - 1, way, way)
    pass_on(half, PLUS, MINUS)

    def finish(hop, way, side):
        line(hop, way, 1 - side).wait_recv()
        relay(hop, way, side).wait_recv()
        for out in both:
            line(hop, way, out).wait_send()
        relay(hop, way, side).wait_send()

    def drain(hop, carry):
        for way in both:
            finish(hop, way, way)
            for stream in range(SIDE + 1):
                ring(stream, way, hop).wait_send()
        return carry

    finish(0, PLUS, PLUS)
    lax.fori_loop(1, half, drain, 0)
    finish(half, PLUS, MINUS)
    for stream in range(SIDE + 1):
        ring(stream, PLUS, half).wait_send()
    for way in both:
        near(way).wait_send()
    near_relay().wait_send()
    keep.wait()


def gather_segments(value):
    rows, width = value.shape
    seg_count = lax.axis_size("seg")
    half = seg_count // SIDE // 2
    dma = pltpu.SemaphoreType.DMA
    return pl.pallas_call(
        gather_kernel,
        out_shape=jax.ShapeDtypeStruct((seg_count, rows, width), value.dtype),
        in_specs=[pl.BlockSpec(memory_space=pltpu.VMEM)],
        out_specs=pl.BlockSpec(memory_space=pltpu.VMEM),
        scratch_shapes=[
            dma,
            dma((3, 2)),
            dma((SIDE + 1, 2, half + 1, 2)),
            dma((half + 1, 2, 2, 2)),
            dma((half + 1, 2, 2)),
        ],
        compiler_params=pltpu.CompilerParams(
            collective_id=0, has_side_effects=True, vmem_limit_bytes=32 * 2**20
        ),
    )(value)


def gram_kernel(rows_each, local_ref, out_ref, parts, sums, peers, reduce_sems, level_sems, share_sems, core_sems):
    sub_count, chunk, _ = parts.shape
    group = peers.shape[0]
    me, seg = lax.axis_index("sub"), lax.axis_index("seg")
    level_count = out_ref.shape[0]
    share = 1.0 / (sub_count * rows_each)

    def ahead(step):
        return lax.rem(me + step, sub_count)

    def partner(mask):
        value = seg
        for bit in range(mask.bit_length()):
            if mask >> bit & 1:
                value = value + 2**bit * (1 - 2 * lax.rem(seg // 2**bit, 2))
        return value

    def rows(device):
        return pl.ds(pl.multiple_of(device * chunk, chunk), chunk)

    def remote(source, target, sems, where):
        return pltpu.make_async_remote_copy(
            src_ref=source,
            dst_ref=target,
            send_sem=sems.at[0],
            recv_sem=sems.at[1],
            device_id=where,
            device_id_type=pl.DeviceIdType.MESH,
        )

    barrier = pltpu.get_barrier_semaphore()
    for step in range(1, sub_count):
        pl.semaphore_signal(
            barrier, inc=1, device_id={"sub": ahead(step)}, device_id_type=pl.DeviceIdType.MESH
        )
    for mask in range(1, group):
        pl.semaphore_signal(
            barrier, inc=1, device_id={"seg": partner(mask)}, device_id_type=pl.DeviceIdType.MESH
        )
    pl.semaphore_wait(barrier, sub_count + group - 2)

    def reduce_copy(step):
        return remote(
            local_ref.at[rows(ahead(step))],
            parts.at[step],
            reduce_sems.at[step],
            {"sub": ahead(step)},
        )

    def level_copy(mask):
        return remote(sums, peers.at[mask], level_sems.at[mask], {"seg": partner(mask)})

    for step in range(1, sub_count):
        reduce_copy(step).start()
    total = local_ref[rows(me), :].astype(jnp.float32)
    for step in range(1, sub_count):
        reduce_copy(step).wait_recv()
        total = total + parts[step].astype(jnp.float32)
    total = total * share
    sums[...] = total.astype(sums.dtype)
    for mask in range(1, group):
        level_copy(mask).start()
    out_ref[0, rows(me), :] = total.astype(out_ref.dtype)
    for level in range(1, level_count):
        for mask in range(2 ** (level - 1), 2**level):
            level_copy(mask).wait_recv()
            total = total + peers[mask].astype(jnp.float32)
        out_ref[level, rows(me), :] = (total * 0.5**level).astype(out_ref.dtype)

    core = lax.rem(me, 2)
    other = me + 1 - 2 * core
    spread = range(2, sub_count, 2)

    def share_copy(step):
        mine = out_ref.at[:, rows(me), :]
        return remote(mine, mine, share_sems.at[step], {"sub": ahead(step)})

    def core_copy(step):
        block = out_ref.at[:, rows(lax.rem(me + sub_count - step, sub_count)), :]
        return remote(block, block, core_sems.at[step], {"sub": other})

    for step in spread:
        share_copy(step).start()
    core_copy(0).start()
    for step in sorted(spread, key=lambda s: min(s, sub_count - s)):
        share_copy(step).wait_recv()
        core_copy(step).start()
    for step in range(0, sub_count, 2):
        core_copy(step).wait_recv()
    for step in range(1, sub_count):
        reduce_copy(step).wait_send()
    for mask in range(1, group):
        level_copy(mask).wait_send()
    for step in spread:
        share_copy(step).wait_send()
    for step in range(0, sub_count, 2):
        core_copy(step).wait_send()


def level_grams(local, rows_each):
    width = local.shape[0]
    sub_count, group = lax.axis_size("sub"), 2**LEVELS
    chunk = width // sub_count
    dma = pltpu.SemaphoreType.DMA
    return pl.pallas_call(
        functools.partial(gram_kernel, rows_each),
        out_shape=jax.ShapeDtypeStruct((LEVELS + 1, width, width), local.dtype),
        in_specs=[pl.BlockSpec(memory_space=pltpu.VMEM)],
        out_specs=pl.BlockSpec(memory_space=pltpu.VMEM),
        scratch_shapes=[
            pltpu.VMEM((sub_count, chunk, width), local.dtype),
            pltpu.VMEM((chunk, width), local.dtype),
            pltpu.VMEM((group, chunk, width), local.dtype),
            dma((sub_count, 2)),
            dma((group, 2)),
            dma((sub_count, 2)),
            dma((sub_count, 2)),
        ],
        compiler_params=pltpu.CompilerParams(collective_id=1, has_side_effects=True),
    )(local)


FAR_UNROLL = 4


def far_kernel(
    source_ref,
    dest_ref,
    position_ref,
    gathered_ref,
    coupling_ref,
    basis_ref,
    block_ref,
    before_ref,
    own_ref,
    after_ref,
    samples_ref,
    gram_ref,
    extended,
):
    leaf_count, rank, leaf_rows = basis_ref.shape
    seg_count = coupling_ref.shape[0]
    slots = coupling_ref.shape[2] // rank
    width = gathered_ref.shape[2]
    near_count = block_ref.shape[1]
    own_rows = own_ref.shape[0]
    for index, part in enumerate((before_ref, own_ref, after_ref)):
        extended[index * own_rows : (index + 1) * own_rows, :] = part[...]
    lane = lax.broadcasted_iota(jnp.int32, (1, slots * rank), 1) // rank

    def step(index, total):
        left, right = [], []
        for part in range(FAR_UNROLL):
            seg = index * FAR_UNROLL + part
            key = jnp.full((1, slots * rank), -1, jnp.int32)
            for slot in range(slots):
                source = source_ref[seg * slots + slot]
                served = jnp.where(source < leaf_count, dest_ref[seg * slots + slot], -1)
                key = jnp.where(lane == slot, served, key)
                start = pl.multiple_of(jnp.minimum(source, leaf_count - 1) * rank, rank)
                right.append(gathered_ref[seg, pl.ds(start, rank), :])
            block = coupling_ref[seg]
            left.append(
                jnp.concatenate(
                    [jnp.where(key == leaf, block, jnp.zeros_like(block)) for leaf in range(leaf_count)],
                    axis=0,
                )
            )
        return total + jnp.dot(
            jnp.concatenate(left, axis=1),
            jnp.concatenate(right, axis=0),
            preferred_element_type=jnp.float32,
        )

    total = lax.fori_loop(
        0, seg_count // FAR_UNROLL, step, jnp.zeros((leaf_count * rank, width), jnp.float32)
    )
    coeff = total.astype(jnp.bfloat16)
    for leaf in range(leaf_count):
        rows = slice(leaf * leaf_rows, (leaf + 1) * leaf_rows)
        far = lax.dot_general(
            basis_ref[leaf],
            coeff[leaf * rank : (leaf + 1) * rank],
            (((0,), (0,)), ((), ())),
            preferred_element_type=jnp.float32,
        )
        picked = []
        for entry in range(near_count):
            position = position_ref[leaf * near_count + entry]
            start = pl.multiple_of(jnp.maximum(position, 0) * leaf_rows, leaf_rows)
            value = extended[pl.ds(start, leaf_rows), :]
            picked.append(jnp.where(position >= 0, value, jnp.zeros_like(value)))
        near = jnp.dot(
            jnp.concatenate([block_ref[leaf, entry] for entry in range(near_count)], axis=1),
            jnp.concatenate(picked, axis=0),
            preferred_element_type=jnp.float32,
        )
        samples_ref[rows, :] = (near + far).astype(jnp.bfloat16)
    samples = samples_ref[...]
    gram_ref[...] = lax.dot_general(
        samples, samples, (((0,), (0,)), ((), ())), preferred_element_type=jnp.float32
    ).astype(gram_ref.dtype)


def far_and_gram(source, dest, position, gathered, coupling, basis, blocks, before, own, after):
    rows, width = own.shape
    smem, vmem = pl.BlockSpec(memory_space=pltpu.SMEM), pl.BlockSpec(memory_space=pltpu.VMEM)
    return pl.pallas_call(
        far_kernel,
        out_shape=(
            jax.ShapeDtypeStruct((rows, width), jnp.bfloat16),
            jax.ShapeDtypeStruct((width, width), jnp.bfloat16),
        ),
        in_specs=[smem] * 3 + [vmem] * 7,
        out_specs=[vmem, vmem],
        scratch_shapes=[pltpu.VMEM((3 * rows, width), own.dtype)],
        compiler_params=pltpu.CompilerParams(vmem_limit_bytes=32 * 2**20),
    )(source, dest, position, gathered, coupling, basis, blocks, before, own, after)


def neighbours(value, axes):
    size = lax.axis_size(axes)
    up = [(i, i + 1) for i in range(size - 1)]
    down = [(j, i) for i, j in up]
    return (lax.ppermute(value, axes, up), lax.ppermute(value, axes, down))


def body(
    near_blocks, sample_cols, near_list, row_basis_t, col_basis_t, couplings, far_source, far_dest
):
    leaf_count, near_count, leaf_rows, _ = near_blocks.shape
    sample_width = sample_cols.shape[1]
    rank_width = row_basis_t.shape[1]
    seg_count = lax.axis_size("seg")
    slot_number_count = far_source.shape[3]
    random_cols = sample_cols.reshape(leaf_count, leaf_rows, sample_width)
    basis_projector = jnp.einsum(
        "jra,jas->jrs", col_basis_t, random_cols, preferred_element_type=jnp.float32
    ).astype(jnp.bfloat16)
    source_rows = jnp.swapaxes(far_source[0, 0], 0, 1).astype(jnp.bfloat16)
    source_rows = jnp.pad(
        source_rows, ((0, 16 - slot_number_count), (0, sample_width - seg_count))
    )
    packed = jnp.concatenate(
        [basis_projector.reshape(leaf_count * rank_width, sample_width), source_rows], axis=0
    )
    gathered = gather_segments(packed)
    sources = gathered[:, leaf_count * rank_width : leaf_count * rank_width + slot_number_count, :]
    sources = lax.dynamic_slice_in_dim(sources, lax.axis_index("seg"), 1, axis=2)
    sources = sources.astype(jnp.int32).reshape(seg_count * slot_number_count)
    before, after = neighbours(sample_cols, ("seg", "sub"))
    base_leaf = (lax.axis_index(("seg", "sub")) - 1) * leaf_count
    position = jnp.where(near_list >= 0, near_list - base_leaf, -1)
    samples, gram_local = far_and_gram(
        sources,
        far_dest.reshape(seg_count * slot_number_count),
        position.reshape(leaf_count * near_count),
        gathered,
        couplings[0, 0],
        row_basis_t,
        near_blocks,
        before,
        sample_cols,
        after,
    )
    segment_factor, transfers = factors(level_grams(gram_local, leaf_count * leaf_rows))
    return (samples, segment_factor, transfers[None])


def solution(mesh):
    in_specs = (
        P(("seg", "sub"), None, None, None),
        P(("seg", "sub"), None),
        P(("seg", "sub"), None),
        P(("seg", "sub"), None, None),
        P(("seg", "sub"), None, None),
        P("seg", "sub", None, None, None),
        P("seg", "sub", None, None),
        P("seg", "sub", None, None),
    )
    out_specs = (P(("seg", "sub"), None), P("seg", None), P("seg", None, None, None))
    return jax.shard_map(body, mesh=mesh, in_specs=in_specs, out_specs=out_specs, check_vma=False)
```

```python
import functools

import jax
import jax.numpy as jnp
from jax import lax
from jax.experimental import pallas as pl
from jax.experimental.pallas import tpu as pltpu
from jax.sharding import PartitionSpec as P

LEVELS = 3

BLOCK = 32
GROUP = 8
PIVOTS = 4


def dot32(a, b, dims):
    return lax.dot_general(
        a, b, (dims, ((), ())), precision=lax.Precision.HIGHEST, preferred_element_type=jnp.float32
    )


def eliminate(blocks):
    size = blocks[0].shape[0]
    rows = lax.broadcasted_iota(jnp.int32, (size, size), 0)
    cols = lax.broadcasted_iota(jnp.int32, (size, size), 1)
    eye = (rows == cols).astype(jnp.float32)
    sub = lax.broadcasted_iota(jnp.int32, (GROUP, 1), 0)
    states = []
    for d in blocks:
        x = jnp.concatenate([d, eye], axis=1)
        states.append([x[g * GROUP : (g + 1) * GROUP] for g in range(size // GROUP)])
    full = (GROUP, 2 * size)
    for k in range(0, size, PIVOTS):
        own, r = divmod(k, GROUP)
        for x in states:
            lines = [jnp.broadcast_to(x[own][r + i : r + i + 1, :], full) for i in range(PIVOTS)]
            held = {
                (i, j): jnp.broadcast_to(x[own][r + i : r + i + 1, k + j : k + j + 1], full)
                for i in range(PIVOTS)
                for j in range(i, PIVOTS)
            }
            columns = [
                [jnp.broadcast_to(x[g][:, k + j : k + j + 1], full) for j in range(PIVOTS)]
                for g in range(own, size // GROUP)
            ]
            for i in range(PIVOTS):
                scale = lax.rsqrt(held[i, i])
                lines[i] = lines[i] * scale
                for j in range(i + 1, PIVOTS):
                    held[i, j] = held[i, j] * scale
                for j in range(i + 1, PIVOTS):
                    lines[j] = lines[j] - held[i, j] * lines[i]
                    for m in range(j, PIVOTS):
                        held[j, m] = held[j, m] - held[i, j] * held[i, m]
                for column in columns:
                    column[i] = column[i] * scale
                    for j in range(i + 1, PIVOTS):
                        column[j] = column[j] - column[i] * held[i, j]
            for g in range(own, size // GROUP):
                below = x[g]
                for i in range(PIVOTS):
                    below = below - columns[g - own][i] * lines[i]
                if g == own:
                    below = jnp.where(sub >= r + PIVOTS, below, x[g])
                    for i in range(PIVOTS):
                        below = jnp.where(sub == r + i, lines[i], below)
                x[g] = below
    out = []
    for x in states:
        x = jnp.concatenate(x, axis=0)
        out.append((jnp.where(rows <= cols, x[:, :size], 0.0), x[:, size:]))
    return out


def factor_kernel(gram_ref, factor_ref, transfer_ref, work, upper):
    count, n, _ = work.shape
    lanes = lax.broadcasted_iota(jnp.int32, (1, n), 1)
    work[...] = gram_ref[...].astype(jnp.float32)
    upper[...] = jnp.zeros_like(upper)
    for at in range(0, n, BLOCK):
        end = at + BLOCK
        inside = (lanes >= at) & (lanes < end)
        pairs = eliminate([work[i, at:end, at:end] for i in range(count)])
        for i in range(count):
            r_block, v_block = pairs[i]
            panel = dot32(v_block, work[i, at:end, :], ((1,), (0,)))
            upper[i, at:end, :] = jnp.where(lanes >= end, panel, 0.0)
            upper[i, at:end, at:end] = r_block
            work[i, at:end, :] = jnp.where(lanes < at, panel, 0.0)
            work[i, at:end, at:end] = v_block
            if end < n:
                step = jnp.where(lanes < at, panel, upper[i, at:end, :])
                step = jnp.where(inside, work[i, at:end, :], step)
                rest = jnp.where(inside, 0.0, work[i, end:, :])
                work[i, end:, :] = rest - dot32(panel[:, end:], step, ((0,), (0,)))
    factor_ref[...] = upper[0]
    for i in range(1, count):
        transfer_ref[i - 1] = dot32(upper[i - 1], work[i], ((1,), (1,))).astype(jnp.bfloat16)


def factors(stacked):
    count, n, _ = stacked.shape
    return pl.pallas_call(
        factor_kernel,
        out_shape=(
            jax.ShapeDtypeStruct((n, n), jnp.float32),
            jax.ShapeDtypeStruct((count - 1, n, n), jnp.bfloat16),
        ),
        in_specs=[pl.BlockSpec(memory_space=pltpu.VMEM)],
        out_specs=[pl.BlockSpec(memory_space=pltpu.VMEM)] * 2,
        scratch_shapes=[
            pltpu.VMEM((count, n, n), jnp.float32),
            pltpu.VMEM((count, n, n), jnp.float32),
        ],
    )(stacked)


SIDE = 4
PLUS, MINUS = 0, 1


def gather_kernel(own_ref, out_ref, own_sem, near_sems, ring_sems, line_sems, relay_sems):
    seg_count, rows, _ = out_ref.shape
    depth = seg_count // SIDE
    half = depth // 2
    me = lax.axis_index("seg")
    z, x = me // SIDE, lax.rem(me, SIDE)
    early = pl.ds(0, rows // 48 * 16)
    late = pl.ds(rows // 48 * 16, rows - rows // 48 * 16)
    sign = (1, -1)
    reach = (half, half - 1)

    def place(dz, dx):
        return lax.rem(z + dz + depth, depth) * SIDE + lax.rem(x + dx + SIDE, SIDE)

    def send(dz, dx, part, sems, target, own):
        source = own_ref.at[part] if own else out_ref.at[place(dz, dx), part]
        return pltpu.make_async_remote_copy(
            src_ref=source,
            dst_ref=out_ref.at[place(dz, dx), part],
            send_sem=sems.at[0],
            recv_sem=sems.at[1],
            device_id={"seg": target},
            device_id_type=pl.DeviceIdType.MESH,
        )

    def along_x(way):
        return place(0, sign[way])

    def along_z(way):
        return place(sign[way], 0)

    def near(way):
        return send(0, 0, early, near_sems.at[way], along_x(way), True)

    def near_relay():
        return send(0, -1, early, near_sems.at[2], along_x(PLUS), False)

    def ring(stream, way, hop, own=False):
        part, dx = (late, 0) if stream == SIDE else (early, stream)
        return send(
            -sign[way] * (hop - 1), dx, part, ring_sems.at[stream, way, hop], along_z(way), own
        )

    def line(hop, way, side, own=False):
        return send(-sign[way] * hop, 0, late, line_sems.at[hop, way, side], along_x(side), own)

    def relay(hop, way, side):
        return send(-sign[way] * hop, -sign[side], late, relay_sems.at[hop, way], along_x(side), False)

    def pass_on(hop, way, side):
        line(hop, way, side).wait_recv()
        relay(hop, way, side).start()

    def advance(stream, way, hop, further):
        ring(stream, way, hop).wait_recv()
        if further:
            ring(stream, way, hop + 1).start()

    def turn(hop, ways, further, streams):
        for way in ways:
            advance(SIDE, way, hop, way in further)
            for side in (PLUS, MINUS):
                line(hop, way, side).start()
        for stream in streams:
            for way in ways:
                advance(stream, way, hop, way in further)

    barrier = pltpu.get_barrier_semaphore()
    for way in (PLUS, MINUS):
        for target in (along_x(way), along_z(way)):
            pl.semaphore_signal(
                barrier, inc=1, device_id={"seg": target}, device_id_type=pl.DeviceIdType.MESH
            )
    pl.semaphore_wait(barrier, 4)

    keep = pltpu.make_async_copy(own_ref, out_ref.at[me], own_sem)
    keep.start()
    for way in (PLUS, MINUS):
        near(way).start()
        ring(SIDE, way, 1, True).start()
    for way in (PLUS, MINUS):
        ring(0, way, 1, True).start()
        line(0, PLUS, way, True).start()
    both = (PLUS, MINUS)
    for way, stream in ((PLUS, SIDE - 1), (MINUS, 1)):
        near(way).wait_recv()
        if way == PLUS:
            near_relay().start()
        for side in both:
            ring(stream, side, 1).start()
    turn(1, both, both, (0, SIDE - 1, 1))
    near_relay().wait_recv()
    for side in both:
        ring(2, side, 1).start()
    pass_on(0, PLUS, PLUS)
    for way in both:
        advance(2, way, 1, True)

    def middle(hop, carry):
        turn(hop, both, both, (0, SIDE - 1, 1, 2))
        for way in both:
            pass_on(hop - 1, way, way)
        return carry

    lax.fori_loop(2, half - 1, middle, 0)
    turn(half - 1, both, (PLUS,), (0, SIDE - 1, 1, 2))
    for way in both:
        pass_on(half - 2, way, way)
    turn(half, (PLUS,), (), (0, SIDE - 1, 1, 2))
    for way in both:
        pass_on(half - 1, way, way)
    pass_on(half, PLUS, MINUS)

    def finish(hop, way, side):
        line(hop, way, 1 - side).wait_recv()
        relay(hop, way, side).wait_recv()
        for out in both:
            line(hop, way, out).wait_send()
        relay(hop, way, side).wait_send()

    def drain(hop, carry):
        for way in both:
            finish(hop, way, way)
            for stream in range(SIDE + 1):
                ring(stream, way, hop).wait_send()
        return carry

    finish(0, PLUS, PLUS)
    lax.fori_loop(1, half, drain, 0)
    finish(half, PLUS, MINUS)
    for stream in range(SIDE + 1):
        ring(stream, PLUS, half).wait_send()
    for way in both:
        near(way).wait_send()
    near_relay().wait_send()
    keep.wait()


def gather_segments(value):
    rows, width = value.shape
    seg_count = lax.axis_size("seg")
    half = seg_count // SIDE // 2
    dma = pltpu.SemaphoreType.DMA
    return pl.pallas_call(
        gather_kernel,
        out_shape=jax.ShapeDtypeStruct((seg_count, rows, width), value.dtype),
        in_specs=[pl.BlockSpec(memory_space=pltpu.VMEM)],
        out_specs=pl.BlockSpec(memory_space=pltpu.VMEM),
        scratch_shapes=[
            dma,
            dma((3, 2)),
            dma((SIDE + 1, 2, half + 1, 2)),
            dma((half + 1, 2, 2, 2)),
            dma((half + 1, 2, 2)),
        ],
        compiler_params=pltpu.CompilerParams(
            collective_id=0, has_side_effects=True, vmem_limit_bytes=32 * 2**20
        ),
    )(value)


def gram_kernel(rows_each, local_ref, out_ref, parts, sums, peers, reduce_sems, level_sems, share_sems, core_sems):
    sub_count, chunk, _ = parts.shape
    group = peers.shape[0]
    me, seg = lax.axis_index("sub"), lax.axis_index("seg")
    level_count = out_ref.shape[0]
    share = 1.0 / (sub_count * rows_each)

    def ahead(step):
        return lax.rem(me + step, sub_count)

    def partner(mask):
        value = seg
        for bit in range(mask.bit_length()):
            if mask >> bit & 1:
                value = value + 2**bit * (1 - 2 * lax.rem(seg // 2**bit, 2))
        return value

    def rows(device):
        return pl.ds(pl.multiple_of(device * chunk, chunk), chunk)

    def remote(source, target, sems, where):
        return pltpu.make_async_remote_copy(
            src_ref=source,
            dst_ref=target,
            send_sem=sems.at[0],
            recv_sem=sems.at[1],
            device_id=where,
            device_id_type=pl.DeviceIdType.MESH,
        )

    barrier = pltpu.get_barrier_semaphore()
    for step in range(1, sub_count):
        pl.semaphore_signal(
            barrier, inc=1, device_id={"sub": ahead(step)}, device_id_type=pl.DeviceIdType.MESH
        )
    for mask in range(1, group):
        pl.semaphore_signal(
            barrier, inc=1, device_id={"seg": partner(mask)}, device_id_type=pl.DeviceIdType.MESH
        )
    pl.semaphore_wait(barrier, sub_count + group - 2)

    def reduce_copy(step):
        return remote(
            local_ref.at[rows(ahead(step))],
            parts.at[step],
            reduce_sems.at[step],
            {"sub": ahead(step)},
        )

    def level_copy(mask):
        return remote(sums, peers.at[mask], level_sems.at[mask], {"seg": partner(mask)})

    for step in range(1, sub_count):
        reduce_copy(step).start()
    total = local_ref[rows(me), :].astype(jnp.float32)
    for step in range(1, sub_count):
        reduce_copy(step).wait_recv()
        total = total + parts[step].astype(jnp.float32)
    total = total * share
    sums[...] = total.astype(sums.dtype)
    for mask in range(1, group):
        level_copy(mask).start()
    out_ref[0, rows(me), :] = total.astype(out_ref.dtype)
    for level in range(1, level_count):
        for mask in range(2 ** (level - 1), 2**level):
            level_copy(mask).wait_recv()
            total = total + peers[mask].astype(jnp.float32)
        out_ref[level, rows(me), :] = (total * 0.5**level).astype(out_ref.dtype)

    core = lax.rem(me, 2)
    other = me + 1 - 2 * core
    spread = range(2, sub_count, 2)

    def share_copy(step):
        mine = out_ref.at[:, rows(me), :]
        return remote(mine, mine, share_sems.at[step], {"sub": ahead(step)})

    def core_copy(step):
        block = out_ref.at[:, rows(lax.rem(me + sub_count - step, sub_count)), :]
        return remote(block, block, core_sems.at[step], {"sub": other})

    for step in spread:
        share_copy(step).start()
    core_copy(0).start()
    for step in sorted(spread, key=lambda s: min(s, sub_count - s)):
        share_copy(step).wait_recv()
        core_copy(step).start()
    for step in range(0, sub_count, 2):
        core_copy(step).wait_recv()
    for step in range(1, sub_count):
        reduce_copy(step).wait_send()
    for mask in range(1, group):
        level_copy(mask).wait_send()
    for step in spread:
        share_copy(step).wait_send()
    for step in range(0, sub_count, 2):
        core_copy(step).wait_send()


def level_grams(local, rows_each):
    width = local.shape[0]
    sub_count, group = lax.axis_size("sub"), 2**LEVELS
    chunk = width // sub_count
    dma = pltpu.SemaphoreType.DMA
    return pl.pallas_call(
        functools.partial(gram_kernel, rows_each),
        out_shape=jax.ShapeDtypeStruct((LEVELS + 1, width, width), local.dtype),
        in_specs=[pl.BlockSpec(memory_space=pltpu.VMEM)],
        out_specs=pl.BlockSpec(memory_space=pltpu.VMEM),
        scratch_shapes=[
            pltpu.VMEM((sub_count, chunk, width), local.dtype),
            pltpu.VMEM((chunk, width), local.dtype),
            pltpu.VMEM((group, chunk, width), local.dtype),
            dma((sub_count, 2)),
            dma((group, 2)),
            dma((sub_count, 2)),
            dma((sub_count, 2)),
        ],
        compiler_params=pltpu.CompilerParams(collective_id=1, has_side_effects=True),
    )(local)


FAR_UNROLL = 4


def far_kernel(
    source_ref,
    dest_ref,
    position_ref,
    gathered_hbm,
    coupling_hbm,
    basis_ref,
    block_ref,
    before_ref,
    own_ref,
    after_ref,
    samples_ref,
    gram_ref,
    extended,
    gathered_ref,
    coupling_ref,
    near_sum,
    sems,
):
    leaf_count, rank, leaf_rows = basis_ref.shape
    seg_count = coupling_ref.shape[0]
    slots = coupling_ref.shape[2] // rank
    width = gathered_ref.shape[2]
    near_count = block_ref.shape[1]
    own_rows = own_ref.shape[0]
    loads = [
        pltpu.make_async_copy(gathered_hbm, gathered_ref, sems.at[0]),
        pltpu.make_async_copy(coupling_hbm, coupling_ref, sems.at[1]),
    ]
    for load in loads:
        load.start()
    for index, part in enumerate((before_ref, own_ref, after_ref)):
        extended[index * own_rows : (index + 1) * own_rows, :] = part[...]
    for leaf in range(leaf_count):
        picked = []
        for entry in range(near_count):
            position = position_ref[leaf, entry]
            start = pl.multiple_of(jnp.maximum(position, 0) * leaf_rows, leaf_rows)
            value = extended[pl.ds(start, leaf_rows), :]
            picked.append(jnp.where(position >= 0, value, jnp.zeros_like(value)))
        near_sum[leaf * leaf_rows : (leaf + 1) * leaf_rows, :] = jnp.dot(
            jnp.concatenate([block_ref[leaf, entry] for entry in range(near_count)], axis=1),
            jnp.concatenate(picked, axis=0),
            preferred_element_type=jnp.float32,
        )
    for load in loads:
        load.wait()
    lane = lax.broadcasted_iota(jnp.int32, (1, slots * rank), 1) // rank

    def step(index, total):
        left, right = [], []
        for part in range(FAR_UNROLL):
            seg = index * FAR_UNROLL + part
            key = jnp.full((1, slots * rank), -1, jnp.int32)
            for slot in range(slots):
                source = source_ref[slot, seg]
                served = jnp.where(source < leaf_count, dest_ref[slot, seg], -1)
                key = jnp.where(lane == slot, served, key)
                start = pl.multiple_of(jnp.minimum(source, leaf_count - 1) * rank, rank)
                right.append(gathered_ref[seg, pl.ds(start, rank), :])
            block = coupling_ref[seg]
            left.append(
                jnp.concatenate(
                    [jnp.where(key == leaf, block, jnp.zeros_like(block)) for leaf in range(leaf_count)],
                    axis=0,
                )
            )
        return total + jnp.dot(
            jnp.concatenate(left, axis=1),
            jnp.concatenate(right, axis=0),
            preferred_element_type=jnp.float32,
        )

    total = lax.fori_loop(
        0, seg_count // FAR_UNROLL, step, jnp.zeros((leaf_count * rank, width), jnp.float32)
    )
    coeff = total.astype(jnp.bfloat16)
    for leaf in range(leaf_count):
        rows = slice(leaf * leaf_rows, (leaf + 1) * leaf_rows)
        far = lax.dot_general(
            basis_ref[leaf],
            coeff[leaf * rank : (leaf + 1) * rank],
            (((0,), (0,)), ((), ())),
            preferred_element_type=jnp.float32,
        )
        samples_ref[rows, :] = (near_sum[rows, :] + far).astype(jnp.bfloat16)
    samples = samples_ref[...]
    gram_ref[...] = lax.dot_general(
        samples, samples, (((0,), (0,)), ((), ())), preferred_element_type=jnp.float32
    ).astype(gram_ref.dtype)


def far_and_gram(source, dest, position, gathered, coupling, basis, blocks, before, own, after):
    rows, width = own.shape
    smem, vmem = pl.BlockSpec(memory_space=pltpu.SMEM), pl.BlockSpec(memory_space=pltpu.VMEM)
    return pl.pallas_call(
        far_kernel,
        out_shape=(
            jax.ShapeDtypeStruct((rows, width), jnp.bfloat16),
            jax.ShapeDtypeStruct((width, width), jnp.bfloat16),
        ),
        in_specs=[smem] * 3 + [pl.BlockSpec(memory_space=pl.ANY)] * 2 + [vmem] * 5,
        out_specs=[vmem, vmem],
        scratch_shapes=[
            pltpu.VMEM((3 * rows, width), own.dtype),
            pltpu.VMEM(gathered.shape, gathered.dtype),
            pltpu.VMEM(coupling.shape, coupling.dtype),
            pltpu.VMEM((rows, width), jnp.float32),
            pltpu.SemaphoreType.DMA((2,)),
        ],
        compiler_params=pltpu.CompilerParams(vmem_limit_bytes=32 * 2**20),
    )(source, dest, position, gathered, coupling, basis, blocks, before, own, after)


def neighbours(value, axes):
    size = lax.axis_size(axes)
    up = [(i, i + 1) for i in range(size - 1)]
    down = [(j, i) for i, j in up]
    return (lax.ppermute(value, axes, up), lax.ppermute(value, axes, down))


def body(
    near_blocks, sample_cols, near_list, row_basis_t, col_basis_t, couplings, far_source, far_dest
):
    leaf_count, near_count, leaf_rows, _ = near_blocks.shape
    sample_width = sample_cols.shape[1]
    rank_width = row_basis_t.shape[1]
    seg_count = lax.axis_size("seg")
    slot_number_count = far_source.shape[3]
    random_cols = sample_cols.reshape(leaf_count, leaf_rows, sample_width)
    basis_projector = jnp.einsum(
        "jra,jas->jrs", col_basis_t, random_cols, preferred_element_type=jnp.float32
    ).astype(jnp.bfloat16)
    source_rows = jnp.swapaxes(far_source[0, 0], 0, 1).astype(jnp.bfloat16)
    source_rows = jnp.pad(
        source_rows, ((0, 16 - slot_number_count), (0, sample_width - seg_count))
    )
    packed = jnp.concatenate(
        [basis_projector.reshape(leaf_count * rank_width, sample_width), source_rows], axis=0
    )
    gathered = gather_segments(packed)
    sources = gathered[:, leaf_count * rank_width : leaf_count * rank_width + slot_number_count, :]
    sources = lax.dynamic_slice_in_dim(sources, lax.axis_index("seg"), 1, axis=2)
    sources = jnp.swapaxes(sources.astype(jnp.int32)[:, :, 0], 0, 1)
    before, after = neighbours(sample_cols, ("seg", "sub"))
    base_leaf = (lax.axis_index(("seg", "sub")) - 1) * leaf_count
    position = jnp.where(near_list >= 0, near_list - base_leaf, -1)
    samples, gram_local = far_and_gram(
        sources,
        jnp.swapaxes(far_dest[0, 0], 0, 1),
        position,
        gathered,
        couplings[0, 0],
        row_basis_t,
        near_blocks,
        before,
        sample_cols,
        after,
    )
    segment_factor, transfers = factors(level_grams(gram_local, leaf_count * leaf_rows))
    return (samples, segment_factor, transfers[None])


def solution(mesh):
    in_specs = (
        P(("seg", "sub"), None, None, None),
        P(("seg", "sub"), None),
        P(("seg", "sub"), None),
        P(("seg", "sub"), None, None),
        P(("seg", "sub"), None, None),
        P("seg", "sub", None, None, None),
        P("seg", "sub", None, None),
        P("seg", "sub", None, None),
    )
    out_specs = (P(("seg", "sub"), None), P("seg", None), P("seg", None, None, None))
    return jax.shard_map(body, mesh=mesh, in_specs=in_specs, out_specs=out_specs, check_vma=False)
```

```python
import functools

import jax
import jax.numpy as jnp
from jax import lax
from jax.experimental import pallas as pl
from jax.experimental.pallas import tpu as pltpu
from jax.sharding import PartitionSpec as P

LEVELS = 3

BLOCK = 32
GROUP = 8
PIVOTS = 4


def dot32(a, b, dims):
    return lax.dot_general(
        a, b, (dims, ((), ())), precision=lax.Precision.HIGHEST, preferred_element_type=jnp.float32
    )


def eliminate(blocks):
    size = blocks[0].shape[0]
    rows = lax.broadcasted_iota(jnp.int32, (size, size), 0)
    cols = lax.broadcasted_iota(jnp.int32, (size, size), 1)
    eye = (rows == cols).astype(jnp.float32)
    sub = lax.broadcasted_iota(jnp.int32, (GROUP, 1), 0)
    states = []
    for d in blocks:
        x = jnp.concatenate([d, eye], axis=1)
        states.append([x[g * GROUP : (g + 1) * GROUP] for g in range(size // GROUP)])
    full = (GROUP, 2 * size)
    for k in range(0, size, PIVOTS):
        own, r = divmod(k, GROUP)
        for x in states:
            lines = [jnp.broadcast_to(x[own][r + i : r + i + 1, :], full) for i in range(PIVOTS)]
            held = {
                (i, j): jnp.broadcast_to(x[own][r + i : r + i + 1, k + j : k + j + 1], full)
                for i in range(PIVOTS)
                for j in range(i, PIVOTS)
            }
            columns = [
                [jnp.broadcast_to(x[g][:, k + j : k + j + 1], full) for j in range(PIVOTS)]
                for g in range(own, size // GROUP)
            ]
            for i in range(PIVOTS):
                scale = lax.rsqrt(held[i, i])
                lines[i] = lines[i] * scale
                for j in range(i + 1, PIVOTS):
                    held[i, j] = held[i, j] * scale
                for j in range(i + 1, PIVOTS):
                    lines[j] = lines[j] - held[i, j] * lines[i]
                    for m in range(j, PIVOTS):
                        held[j, m] = held[j, m] - held[i, j] * held[i, m]
                for column in columns:
                    column[i] = column[i] * scale
                    for j in range(i + 1, PIVOTS):
                        column[j] = column[j] - column[i] * held[i, j]
            for g in range(own, size // GROUP):
                below = x[g]
                for i in range(PIVOTS):
                    below = below - columns[g - own][i] * lines[i]
                if g == own:
                    below = jnp.where(sub >= r + PIVOTS, below, x[g])
                    for i in range(PIVOTS):
                        below = jnp.where(sub == r + i, lines[i], below)
                x[g] = below
    out = []
    for x in states:
        x = jnp.concatenate(x, axis=0)
        out.append((jnp.where(rows <= cols, x[:, :size], 0.0), x[:, size:]))
    return out


def factor_kernel(gram_ref, factor_ref, transfer_ref, work, upper):
    count, n, _ = work.shape
    lanes = lax.broadcasted_iota(jnp.int32, (1, n), 1)
    work[...] = gram_ref[...].astype(jnp.float32)
    upper[...] = jnp.zeros_like(upper)
    for at in range(0, n, BLOCK):
        end = at + BLOCK
        inside = (lanes >= at) & (lanes < end)
        pairs = eliminate([work[i, at:end, at:end] for i in range(count)])
        for i in range(count):
            r_block, v_block = pairs[i]
            panel = dot32(v_block, work[i, at:end, :], ((1,), (0,)))
            upper[i, at:end, :] = jnp.where(lanes >= end, panel, 0.0)
            upper[i, at:end, at:end] = r_block
            work[i, at:end, :] = jnp.where(lanes < at, panel, 0.0)
            work[i, at:end, at:end] = v_block
            if end < n:
                step = jnp.where(lanes < at, panel, upper[i, at:end, :])
                step = jnp.where(inside, work[i, at:end, :], step)
                rest = jnp.where(inside, 0.0, work[i, end:, :])
                work[i, end:, :] = rest - dot32(panel[:, end:], step, ((0,), (0,)))
    factor_ref[...] = upper[0]
    for i in range(1, count):
        transfer_ref[i - 1] = dot32(upper[i - 1], work[i], ((1,), (1,))).astype(jnp.bfloat16)


def factors(stacked):
    count, n, _ = stacked.shape
    return pl.pallas_call(
        factor_kernel,
        out_shape=(
            jax.ShapeDtypeStruct((n, n), jnp.float32),
            jax.ShapeDtypeStruct((count - 1, n, n), jnp.bfloat16),
        ),
        in_specs=[pl.BlockSpec(memory_space=pltpu.VMEM)],
        out_specs=[pl.BlockSpec(memory_space=pltpu.VMEM)] * 2,
        scratch_shapes=[
            pltpu.VMEM((count, n, n), jnp.float32),
            pltpu.VMEM((count, n, n), jnp.float32),
        ],
    )(stacked)


SIDE = 4
PLUS, MINUS = 0, 1


def gather_kernel(own_ref, out_ref, own_sem, near_sems, ring_sems, line_sems, relay_sems):
    seg_count, rows, _ = out_ref.shape
    depth = seg_count // SIDE
    half = depth // 2
    me = lax.axis_index("seg")
    z, x = me // SIDE, lax.rem(me, SIDE)
    early = pl.ds(0, rows // 48 * 16)
    late = pl.ds(rows // 48 * 16, rows - rows // 48 * 16)
    sign = (1, -1)
    reach = (half, half - 1)

    def place(dz, dx):
        return lax.rem(z + dz + depth, depth) * SIDE + lax.rem(x + dx + SIDE, SIDE)

    def send(dz, dx, part, sems, target, own):
        source = own_ref.at[part] if own else out_ref.at[place(dz, dx), part]
        return pltpu.make_async_remote_copy(
            src_ref=source,
            dst_ref=out_ref.at[place(dz, dx), part],
            send_sem=sems.at[0],
            recv_sem=sems.at[1],
            device_id={"seg": target},
            device_id_type=pl.DeviceIdType.MESH,
        )

    def along_x(way):
        return place(0, sign[way])

    def along_z(way):
        return place(sign[way], 0)

    def near(way):
        return send(0, 0, early, near_sems.at[way], along_x(way), True)

    def near_relay():
        return send(0, -1, early, near_sems.at[2], along_x(PLUS), False)

    def ring(stream, way, hop, own=False):
        part, dx = (late, 0) if stream == SIDE else (early, stream)
        return send(
            -sign[way] * (hop - 1), dx, part, ring_sems.at[stream, way, hop], along_z(way), own
        )

    def line(hop, way, side, own=False):
        return send(-sign[way] * hop, 0, late, line_sems.at[hop, way, side], along_x(side), own)

    def relay(hop, way, side):
        return send(-sign[way] * hop, -sign[side], late, relay_sems.at[hop, way], along_x(side), False)

    def pass_on(hop, way, side):
        line(hop, way, side).wait_recv()
        relay(hop, way, side).start()

    def advance(stream, way, hop, further):
        ring(stream, way, hop).wait_recv()
        if further:
            ring(stream, way, hop + 1).start()

    def turn(hop, ways, further, streams):
        for way in ways:
            advance(SIDE, way, hop, way in further)
            for side in (PLUS, MINUS):
                line(hop, way, side).start()
        for stream in streams:
            for way in ways:
                advance(stream, way, hop, way in further)

    barrier = pltpu.get_barrier_semaphore()
    for way in (PLUS, MINUS):
        for target in (along_x(way), along_z(way)):
            pl.semaphore_signal(
                barrier, inc=1, device_id={"seg": target}, device_id_type=pl.DeviceIdType.MESH
            )
    pl.semaphore_wait(barrier, 4)

    keep = pltpu.make_async_copy(own_ref, out_ref.at[me], own_sem)
    keep.start()
    for way in (PLUS, MINUS):
        near(way).start()
        ring(SIDE, way, 1, True).start()
    for way in (PLUS, MINUS):
        ring(0, way, 1, True).start()
        line(0, PLUS, way, True).start()
    both = (PLUS, MINUS)
    for way, stream in ((PLUS, SIDE - 1), (MINUS, 1)):
        near(way).wait_recv()
        if way == PLUS:
            near_relay().start()
        for side in both:
            ring(stream, side, 1).start()
    turn(1, both, both, (0, SIDE - 1, 1))
    near_relay().wait_recv()
    for side in both:
        ring(2, side, 1).start()
    pass_on(0, PLUS, PLUS)
    for way in both:
        advance(2, way, 1, True)

    def middle(hop, carry):
        turn(hop, both, both, (0, SIDE - 1, 1, 2))
        for way in both:
            pass_on(hop - 1, way, way)
        return carry

    lax.fori_loop(2, half - 1, middle, 0)
    turn(half - 1, both, (PLUS,), (0, SIDE - 1, 1, 2))
    for way in both:
        pass_on(half - 2, way, way)
    turn(half, (PLUS,), (), (0, SIDE - 1, 1, 2))
    for way in both:
        pass_on(half - 1, way, way)
    pass_on(half, PLUS, MINUS)

    def finish(hop, way, side):
        line(hop, way, 1 - side).wait_recv()
        relay(hop, way, side).wait_recv()
        for out in both:
            line(hop, way, out).wait_send()
        relay(hop, way, side).wait_send()

    def drain(hop, carry):
        for way in both:
            finish(hop, way, way)
            for stream in range(SIDE + 1):
                ring(stream, way, hop).wait_send()
        return carry

    finish(0, PLUS, PLUS)
    lax.fori_loop(1, half, drain, 0)
    finish(half, PLUS, MINUS)
    for stream in range(SIDE + 1):
        ring(stream, PLUS, half).wait_send()
    for way in both:
        near(way).wait_send()
    near_relay().wait_send()
    keep.wait()


def gather_segments(value):
    rows, width = value.shape
    seg_count = lax.axis_size("seg")
    half = seg_count // SIDE // 2
    dma = pltpu.SemaphoreType.DMA
    return pl.pallas_call(
        gather_kernel,
        out_shape=jax.ShapeDtypeStruct((seg_count, rows, width), value.dtype),
        in_specs=[pl.BlockSpec(memory_space=pltpu.VMEM)],
        out_specs=pl.BlockSpec(memory_space=pl.ANY),
        scratch_shapes=[
            dma,
            dma((3, 2)),
            dma((SIDE + 1, 2, half + 1, 2)),
            dma((half + 1, 2, 2, 2)),
            dma((half + 1, 2, 2)),
        ],
        compiler_params=pltpu.CompilerParams(
            collective_id=0, has_side_effects=True, vmem_limit_bytes=56 * 2**20
        ),
    )(value)


def gram_kernel(rows_each, local_ref, out_ref, parts, sums, peers, reduce_sems, level_sems, share_sems, core_sems):
    sub_count, chunk, _ = parts.shape
    group = peers.shape[0]
    me, seg = lax.axis_index("sub"), lax.axis_index("seg")
    level_count = out_ref.shape[0]
    share = 1.0 / (sub_count * rows_each)

    def ahead(step):
        return lax.rem(me + step, sub_count)

    def partner(mask):
        value = seg
        for bit in range(mask.bit_length()):
            if mask >> bit & 1:
                value = value + 2**bit * (1 - 2 * lax.rem(seg // 2**bit, 2))
        return value

    def rows(device):
        return pl.ds(pl.multiple_of(device * chunk, chunk), chunk)

    def remote(source, target, sems, where):
        return pltpu.make_async_remote_copy(
            src_ref=source,
            dst_ref=target,
            send_sem=sems.at[0],
            recv_sem=sems.at[1],
            device_id=where,
            device_id_type=pl.DeviceIdType.MESH,
        )

    barrier = pltpu.get_barrier_semaphore()
    for step in range(1, sub_count):
        pl.semaphore_signal(
            barrier, inc=1, device_id={"sub": ahead(step)}, device_id_type=pl.DeviceIdType.MESH
        )
    for mask in range(1, group):
        pl.semaphore_signal(
            barrier, inc=1, device_id={"seg": partner(mask)}, device_id_type=pl.DeviceIdType.MESH
        )
    pl.semaphore_wait(barrier, sub_count + group - 2)

    def reduce_copy(step):
        return remote(
            local_ref.at[rows(ahead(step))],
            parts.at[step],
            reduce_sems.at[step],
            {"sub": ahead(step)},
        )

    def level_copy(mask):
        return remote(sums, peers.at[mask], level_sems.at[mask], {"seg": partner(mask)})

    for step in range(1, sub_count):
        reduce_copy(step).start()
    total = local_ref[rows(me), :].astype(jnp.float32)
    for step in range(1, sub_count):
        reduce_copy(step).wait_recv()
        total = total + parts[step].astype(jnp.float32)
    total = total * share
    sums[...] = total.astype(sums.dtype)
    for mask in range(1, group):
        level_copy(mask).start()
    out_ref[0, rows(me), :] = total.astype(out_ref.dtype)
    for level in range(1, level_count):
        for mask in range(2 ** (level - 1), 2**level):
            level_copy(mask).wait_recv()
            total = total + peers[mask].astype(jnp.float32)
        out_ref[level, rows(me), :] = (total * 0.5**level).astype(out_ref.dtype)

    core = lax.rem(me, 2)
    other = me + 1 - 2 * core
    spread = range(2, sub_count, 2)

    def share_copy(step):
        mine = out_ref.at[:, rows(me), :]
        return remote(mine, mine, share_sems.at[step], {"sub": ahead(step)})

    def core_copy(step):
        block = out_ref.at[:, rows(lax.rem(me + sub_count - step, sub_count)), :]
        return remote(block, block, core_sems.at[step], {"sub": other})

    for step in spread:
        share_copy(step).start()
    core_copy(0).start()
    for step in sorted(spread, key=lambda s: min(s, sub_count - s)):
        share_copy(step).wait_recv()
        core_copy(step).start()
    for step in range(0, sub_count, 2):
        core_copy(step).wait_recv()
    for step in range(1, sub_count):
        reduce_copy(step).wait_send()
    for mask in range(1, group):
        level_copy(mask).wait_send()
    for step in spread:
        share_copy(step).wait_send()
    for step in range(0, sub_count, 2):
        core_copy(step).wait_send()


def level_grams(local, rows_each):
    width = local.shape[0]
    sub_count, group = lax.axis_size("sub"), 2**LEVELS
    chunk = width // sub_count
    dma = pltpu.SemaphoreType.DMA
    return pl.pallas_call(
        functools.partial(gram_kernel, rows_each),
        out_shape=jax.ShapeDtypeStruct((LEVELS + 1, width, width), local.dtype),
        in_specs=[pl.BlockSpec(memory_space=pltpu.VMEM)],
        out_specs=pl.BlockSpec(memory_space=pltpu.VMEM),
        scratch_shapes=[
            pltpu.VMEM((sub_count, chunk, width), local.dtype),
            pltpu.VMEM((chunk, width), local.dtype),
            pltpu.VMEM((group, chunk, width), local.dtype),
            dma((sub_count, 2)),
            dma((group, 2)),
            dma((sub_count, 2)),
            dma((sub_count, 2)),
        ],
        compiler_params=pltpu.CompilerParams(collective_id=1, has_side_effects=True),
    )(local)


FAR_UNROLL = 4


def far_kernel(
    source_ref,
    dest_ref,
    position_ref,
    gathered_hbm,
    coupling_hbm,
    basis_ref,
    block_ref,
    before_ref,
    own_ref,
    after_ref,
    samples_ref,
    gram_ref,
    extended,
    gathered_ref,
    coupling_ref,
    near_sum,
    sems,
):
    leaf_count, rank, leaf_rows = basis_ref.shape
    seg_count = coupling_ref.shape[0]
    slots = coupling_ref.shape[2] // rank
    width = gathered_ref.shape[2]
    near_count = block_ref.shape[1]
    own_rows = own_ref.shape[0]
    loads = [
        pltpu.make_async_copy(gathered_hbm, gathered_ref, sems.at[0]),
        pltpu.make_async_copy(coupling_hbm, coupling_ref, sems.at[1]),
    ]
    for load in loads:
        load.start()
    for index, part in enumerate((before_ref, own_ref, after_ref)):
        extended[index * own_rows : (index + 1) * own_rows, :] = part[...]
    for leaf in range(leaf_count):
        picked = []
        for entry in range(near_count):
            position = position_ref[leaf, entry]
            start = pl.multiple_of(jnp.maximum(position, 0) * leaf_rows, leaf_rows)
            value = extended[pl.ds(start, leaf_rows), :]
            picked.append(jnp.where(position >= 0, value, jnp.zeros_like(value)))
        near_sum[leaf * leaf_rows : (leaf + 1) * leaf_rows, :] = jnp.dot(
            jnp.concatenate([block_ref[leaf, entry] for entry in range(near_count)], axis=1),
            jnp.concatenate(picked, axis=0),
            preferred_element_type=jnp.float32,
        )
    for load in loads:
        load.wait()
    lane = lax.broadcasted_iota(jnp.int32, (1, slots * rank), 1) // rank

    def step(index, total):
        left, right = [], []
        for part in range(FAR_UNROLL):
            seg = index * FAR_UNROLL + part
            key = jnp.full((1, slots * rank), -1, jnp.int32)
            for slot in range(slots):
                source = source_ref[slot, seg]
                served = jnp.where(source < leaf_count, dest_ref[slot, seg], -1)
                key = jnp.where(lane == slot, served, key)
                start = pl.multiple_of(jnp.minimum(source, leaf_count - 1) * rank, rank)
                right.append(gathered_ref[seg, pl.ds(start, rank), :])
            block = coupling_ref[seg]
            left.append(
                jnp.concatenate(
                    [jnp.where(key == leaf, block, jnp.zeros_like(block)) for leaf in range(leaf_count)],
                    axis=0,
                )
            )
        return total + jnp.dot(
            jnp.concatenate(left, axis=1),
            jnp.concatenate(right, axis=0),
            preferred_element_type=jnp.float32,
        )

    total = lax.fori_loop(
        0, seg_count // FAR_UNROLL, step, jnp.zeros((leaf_count * rank, width), jnp.float32)
    )
    coeff = total.astype(jnp.bfloat16)
    for leaf in range(leaf_count):
        rows = slice(leaf * leaf_rows, (leaf + 1) * leaf_rows)
        far = lax.dot_general(
            basis_ref[leaf],
            coeff[leaf * rank : (leaf + 1) * rank],
            (((0,), (0,)), ((), ())),
            preferred_element_type=jnp.float32,
        )
        samples_ref[rows, :] = (near_sum[rows, :] + far).astype(jnp.bfloat16)
    samples = samples_ref[...]
    gram_ref[...] = lax.dot_general(
        samples, samples, (((0,), (0,)), ((), ())), preferred_element_type=jnp.float32
    ).astype(gram_ref.dtype)


def far_and_gram(source, dest, position, gathered, coupling, basis, blocks, before, own, after):
    rows, width = own.shape
    smem, vmem = pl.BlockSpec(memory_space=pltpu.SMEM), pl.BlockSpec(memory_space=pltpu.VMEM)
    return pl.pallas_call(
        far_kernel,
        out_shape=(
            jax.ShapeDtypeStruct((rows, width), jnp.bfloat16),
            jax.ShapeDtypeStruct((width, width), jnp.bfloat16),
        ),
        in_specs=[smem] * 3 + [pl.BlockSpec(memory_space=pl.ANY)] * 2 + [vmem] * 5,
        out_specs=[vmem, vmem],
        scratch_shapes=[
            pltpu.VMEM((3 * rows, width), own.dtype),
            pltpu.VMEM(gathered.shape, gathered.dtype),
            pltpu.VMEM(coupling.shape, coupling.dtype),
            pltpu.VMEM((rows, width), jnp.float32),
            pltpu.SemaphoreType.DMA((2,)),
        ],
        compiler_params=pltpu.CompilerParams(vmem_limit_bytes=56 * 2**20),
    )(source, dest, position, gathered, coupling, basis, blocks, before, own, after)


def neighbours(value, axes):
    size = lax.axis_size(axes)
    up = [(i, i + 1) for i in range(size - 1)]
    down = [(j, i) for i, j in up]
    return (lax.ppermute(value, axes, up), lax.ppermute(value, axes, down))


def body(
    near_blocks, sample_cols, near_list, row_basis_t, col_basis_t, couplings, far_source, far_dest
):
    leaf_count, near_count, leaf_rows, _ = near_blocks.shape
    sample_width = sample_cols.shape[1]
    rank_width = row_basis_t.shape[1]
    seg_count = lax.axis_size("seg")
    slot_number_count = far_source.shape[3]
    random_cols = sample_cols.reshape(leaf_count, leaf_rows, sample_width)
    basis_projector = jnp.einsum(
        "jra,jas->jrs", col_basis_t, random_cols, preferred_element_type=jnp.float32
    ).astype(jnp.bfloat16)
    source_rows = jnp.swapaxes(far_source[0, 0], 0, 1).astype(jnp.bfloat16)
    source_rows = jnp.pad(
        source_rows, ((0, 16 - slot_number_count), (0, sample_width - seg_count))
    )
    packed = jnp.concatenate(
        [basis_projector.reshape(leaf_count * rank_width, sample_width), source_rows], axis=0
    )
    gathered = gather_segments(packed)
    sources = gathered[:, leaf_count * rank_width : leaf_count * rank_width + slot_number_count, :]
    sources = lax.dynamic_slice_in_dim(sources, lax.axis_index("seg"), 1, axis=2)
    sources = jnp.swapaxes(sources.astype(jnp.int32)[:, :, 0], 0, 1)
    before, after = neighbours(sample_cols, ("seg", "sub"))
    base_leaf = (lax.axis_index(("seg", "sub")) - 1) * leaf_count
    position = jnp.where(near_list >= 0, near_list - base_leaf, -1)
    samples, gram_local = far_and_gram(
        sources,
        jnp.swapaxes(far_dest[0, 0], 0, 1),
        position,
        gathered,
        couplings[0, 0],
        row_basis_t,
        near_blocks,
        before,
        sample_cols,
        after,
    )
    segment_factor, transfers = factors(level_grams(gram_local, leaf_count * leaf_rows))
    return (samples, segment_factor, transfers[None])


def solution(mesh):
    in_specs = (
        P(("seg", "sub"), None, None, None),
        P(("seg", "sub"), None),
        P(("seg", "sub"), None),
        P(("seg", "sub"), None, None),
        P(("seg", "sub"), None, None),
        P("seg", "sub", None, None, None),
        P("seg", "sub", None, None),
        P("seg", "sub", None, None),
    )
    out_specs = (P(("seg", "sub"), None), P("seg", None), P("seg", None, None, None))
    return jax.shard_map(body, mesh=mesh, in_specs=in_specs, out_specs=out_specs, check_vma=False)
```
